32 devices in a mesh: group: 4 (over y, x), tensor: 8 (over z, core).
Axes of the slice: x: 2, y: 2, z: 4, core: 2. Of those that a mesh axis runs over, the one named last changes fastest.
Arguments:
- prefill_states: bfloat16 [16384, 8192], P('group', 'tensor'), may hold values from -6 to 6
- key_weight: bfloat16 [8192, 1024], P('tensor'), may hold values from -0.0625 to 0.0625
- value_weight: bfloat16 [8192, 1024], P('tensor'), may hold values from -0.0625 to 0.0625
- page_slot: int32 [4, 8, 64], P('group', 'tensor'), may hold values from 0 to 63, each once within a row
- decode_states: bfloat16 [16, 8192], P('group'), may hold values from -6 to 6
- query_weight: bfloat16 [8192, 8192], P(None, 'tensor'), may hold values from -0.0625 to 0.0625
- cache_keys: bfloat16 [16, 4096, 1024], P('group', 'tensor'), may hold values from -606 to 606
- cache_values: bfloat16 [16, 4096, 1024], P('group', 'tensor'), may hold values from -6 to 6
- cached_length: int32 [16], P('group'), may hold values from 1 to 4096
Outputs:
- attention_out: bfloat16 [16, 8192], P('group', 'tensor')
The draws below stay inside these ranges and needn't reach their ends.
Inputs may be any that keep to these rules, and one draw needn't show every extreme that they name: For every group g and block t, page_slot[g, t, :] is a permutation of 0 to 63.
All inputs are finite; a program needn't handle non-finite values.
Results may differ from the reference program's by a relative error of at most 0.017.
Values may be sent and summed in bfloat16 or wider, within the bound.
A program may use at most 192 MiB of HBM per device.

```python
import jax
import jax.numpy as jnp
from jax import lax

D = 8192
QUERY_HEAD_COUNT = 64
KEY_VALUE_HEADS = 8
HEAD_WIDTH = 128
PAGE = 8
PRE_TOK = 4096
B_DEV = 4
KVW = 1024
QW = 8192
GROUPS = 4
RANKS = 8
PRE_ALL = 16384
DECODE_BATCH = 16
CONTEXT = 4096
PAGES_DEV = 64
PER_OWNER = 16
FRESH_ROW = 128
N_GROUP = 4
N_TENSOR = 8


def draw_cache_keys(key, part):
    normal_key = jax.random.fold_in(key, 0)
    base_draw = jnp.clip(jax.random.normal(normal_key, (DECODE_BATCH, CONTEXT, KVW), jnp.float32), -6.0, 6.0)
    return base_draw.astype(jnp.bfloat16)


def set_ends(values, key, low, top_value):
    shape = values.shape
    spot = [jax.random.randint(jax.random.fold_in(key, axis), (), 0, shape[axis]) for axis in range(len(shape))]
    values = values.at[tuple(spot)].set(low)
    longest = shape.index(max(shape))
    spot[longest] = (spot[longest] + 1) % shape[longest]
    return values.at[tuple(spot)].set(top_value)


def block_scale(rng, shape, pieces, smallest, high):
    factor_of, own = 1.0, jax.random.fold_in(rng, 6)
    for position, parts in pieces:
        heights = jnp.exp(jax.random.uniform(jax.random.fold_in(own, position), (parts,), jnp.float32, smallest / len(pieces), high / len(pieces)))
        factor_of = factor_of * jnp.repeat(heights, shape[position] // parts).reshape([-1 if axis == position else 1 for axis in range(len(shape))])
    return factor_of


def bell_draw(key, extent, width, reach, pieces=(), kind=jnp.bfloat16):
    result = jax.random.normal(key, extent, jnp.float32) * width
    if len(pieces) > 0:
        result = block_scale(key, extent, pieces, -0.22, 0.18) * result
    return jnp.clip(result, min=-reach, max=reach).astype(kind)


def setup_inputs(seed: int = 0) -> dict:
    arg_keys = jax.random.split(jax.random.key(seed), 10)
    return {
        "prefill_states": bell_draw(arg_keys[0], (PRE_ALL, D), 1.0, 6.0, ((0, 4), (1, 8))),
        "key_weight": bell_draw(arg_keys[1], (D, KVW), D ** -0.5, 0.0625, ((0, 8),)),
        "value_weight": bell_draw(arg_keys[2], (D, KVW), D ** -0.5, 0.0625, ((0, 8),)),
        "page_slot": jax.vmap(lambda own: jax.random.permutation(own, PAGES_DEV))(jax.random.split(arg_keys[3], GROUPS * RANKS)).reshape((GROUPS, RANKS, PAGES_DEV)).astype(jnp.int32),
        "decode_states": bell_draw(arg_keys[4], (DECODE_BATCH, D), 1.0, 6.0, ((0, 4),)),
        "query_weight": bell_draw(arg_keys[5], (D, QW), D ** -0.5, 0.0625, ((1, 8),)),
        "cache_keys": draw_cache_keys(jax.random.fold_in(arg_keys[9], 71), 0),
        "cache_values": bell_draw(arg_keys[7], (DECODE_BATCH, CONTEXT, KVW), 1.0, 6.0, ((0, 4), (1, 8))),
        "cached_length": set_ends(jax.random.randint(arg_keys[8], (DECODE_BATCH,), 1, CONTEXT + 1), jax.random.fold_in(arg_keys[8], 1), 1, CONTEXT).astype(jnp.int32),
    }


rope_theta = 500000.0
masked_score = -1e30


def apply_rotary(vectors, positions):
    half_width = vectors.shape[-1] // 2
    index_float = jnp.arange(half_width, dtype=jnp.float32)
    frequency = rope_theta ** (-2.0 * index_float / vectors.shape[-1])
    angles = positions[..., None].astype(jnp.float32) * frequency
    cosine_part = jnp.cos(angles)
    sine_part = jnp.sin(angles)
    first_half = vectors[..., :half_width]
    second_half = vectors[..., half_width:]
    return jnp.concatenate([first_half * cosine_part - second_half * sine_part, second_half * cosine_part + first_half * sine_part], axis=-1)


def reference(prefill_states, key_weight, value_weight, page_slot, decode_states, query_weight, cache_keys, cache_values, cached_length):
    def project(states):
        key_proj = jnp.dot(states, key_weight, preferred_element_type=jnp.float32)
        value_proj = jnp.dot(states, value_weight, preferred_element_type=jnp.float32)
        return key_proj.astype(jnp.bfloat16), value_proj.astype(jnp.bfloat16)

    fresh_keys, fresh_values = lax.map(project, prefill_states.reshape(N_GROUP, PRE_TOK, D))
    inverse = jnp.argsort(page_slot, axis=-1).astype(jnp.int32)

    def to_owners(fresh_rows):
        page_blocks = fresh_rows.reshape(N_GROUP, N_TENSOR, PAGES_DEV, PAGE * KVW)
        ordered = jnp.take_along_axis(page_blocks, inverse[..., None], axis=2)
        ordered = ordered.reshape(N_GROUP, N_TENSOR, N_GROUP, PER_OWNER * PAGE * KVW).transpose(2, 1, 0, 3)
        ordered = ordered.reshape(N_GROUP, N_TENSOR, B_DEV, FRESH_ROW, KVW).transpose(0, 2, 1, 3, 4)
        return ordered.reshape(DECODE_BATCH, N_TENSOR * FRESH_ROW, KVW)

    keys_in_place = to_owners(fresh_keys)
    owner_values = to_owners(fresh_values)
    fresh_length = N_TENSOR * FRESH_ROW
    fresh_position_index = cached_length[:, None] + jnp.arange(fresh_length, dtype=jnp.int32)[None, :]
    keys_by_owner = apply_rotary(keys_in_place.astype(jnp.float32).reshape(DECODE_BATCH, fresh_length, KEY_VALUE_HEADS, HEAD_WIDTH), fresh_position_index[:, :, None])
    keys_by_owner = keys_by_owner.reshape(DECODE_BATCH, fresh_length, KVW).astype(jnp.bfloat16)
    query_vectors = jnp.dot(decode_states, query_weight, preferred_element_type=jnp.float32).reshape(DECODE_BATCH, QUERY_HEAD_COUNT, HEAD_WIDTH)
    query_vectors = apply_rotary(query_vectors, (cached_length + fresh_length)[:, None]).astype(jnp.bfloat16).reshape(DECODE_BATCH, KEY_VALUE_HEADS, QUERY_HEAD_COUNT // KEY_VALUE_HEADS, HEAD_WIDTH)

    def attend(inputs):
        query_row, prior_keys, prior_values, incoming_keys, incoming_values, length = inputs
        key_row_block = jnp.concatenate([prior_keys, incoming_keys], axis=0).reshape(-1, KEY_VALUE_HEADS, HEAD_WIDTH).astype(jnp.float32)
        value_row_block = jnp.concatenate([prior_values, incoming_values], axis=0).reshape(-1, KEY_VALUE_HEADS, HEAD_WIDTH).astype(jnp.float32)
        scores = jnp.einsum("hgd,lhd->hgl", query_row.astype(jnp.float32), key_row_block) / (HEAD_WIDTH ** 0.5)
        usable = jnp.concatenate([jnp.arange(CONTEXT, dtype=jnp.int32) < length, jnp.ones((fresh_length,), dtype=bool)])
        scores = jnp.where(usable, scores, masked_score)
        row_peak = jnp.max(scores, axis=-1, keepdims=True)
        weights = jnp.exp(scores - row_peak)
        row_total = jnp.sum(weights, axis=-1)
        rounded = lax.optimization_barrier(weights.astype(jnp.bfloat16)).astype(jnp.float32)
        blended = jnp.einsum("hgl,lhd->hgd", rounded, value_row_block) / row_total[..., None]
        return blended.reshape(QW).astype(jnp.bfloat16)

    return lax.map(attend, (query_vectors, cache_keys, cache_values, keys_by_owner, owner_values, cached_length))
```

```python
import functools

import jax
import jax.numpy as jnp
from jax import lax
from jax.experimental import pallas as pl
from jax.experimental.pallas import tpu as pltpu
from jax.sharding import PartitionSpec as P

HEAD_WIDTH = 128
PAGE = 8


rope_theta = 500000.0
masked_score = -1e30


def angles_of(positions):
    half_width = HEAD_WIDTH // 2
    index_float = jnp.arange(half_width, dtype=jnp.float32)
    frequency = rope_theta ** (-2.0 * index_float / HEAD_WIDTH)
    return positions[..., None].astype(jnp.float32) * frequency


def full_tables(positions):
    angles = angles_of(positions)
    cosine_part = jnp.cos(angles)
    sine_part = jnp.sin(angles)
    return (
        jnp.concatenate([cosine_part, cosine_part], axis=-1),
        jnp.concatenate([sine_part, sine_part], axis=-1),
    )


def apply_rotary(vectors, positions):
    half_width = vectors.shape[-1] // 2
    angles = angles_of(positions)
    cosine_part = jnp.cos(angles)
    sine_part = jnp.sin(angles)
    first_half = vectors[..., :half_width]
    second_half = vectors[..., half_width:]
    return jnp.concatenate(
        [
            first_half * cosine_part - second_half * sine_part,
            second_half * cosine_part + first_half * sine_part,
        ],
        axis=-1,
    )


def score_kernel(
    blocks, owners, order, x_ref, weight, queries, base_cos, base_sin, step_cos, step_sin,
    scores, sorted_x, held, sems,
):
    block = pl.program_id(0)
    fresh_count = held.shape[1]
    pages = fresh_count // PAGE
    share = fresh_count // owners
    kv_heads = weight.shape[1] // HEAD_WIDTH

    def fetch(which, slot):
        def one(s, carry):
            page = order[which * pages + s]
            start = pl.multiple_of(which * fresh_count + page * PAGE, PAGE)
            pltpu.make_async_copy(
                x_ref.at[pl.ds(start, PAGE), :],
                held.at[slot, pl.ds(pl.multiple_of(s * PAGE, PAGE), PAGE), :],
                sems.at[slot],
            ).start()
            return carry

        lax.fori_loop(0, pages, one, 0, unroll=8)

    slot = lax.rem(block, 2)

    @pl.when(block == 0)
    def _():
        fetch(0, 0)

    @pl.when(block + 1 < blocks)
    def _():
        fetch(block + 1, 1 - slot)

    pltpu.make_async_copy(x_ref.at[pl.ds(0, fresh_count), :], held.at[slot], sems.at[slot]).wait()
    x = held[slot]
    sorted_x[...] = x
    lane = lax.broadcasted_iota(jnp.int32, (share, HEAD_WIDTH), 1)
    sign = jnp.where(lane < HEAD_WIDTH // 2, -1.0, 1.0).astype(jnp.float32)
    small_cos, small_sin = step_cos[...], step_sin[...]
    for o in range(owners):
        rows = slice(o * share, (o + 1) * share)
        keys = jnp.dot(x[rows], weight[...], preferred_element_type=jnp.float32)
        big_cos = base_cos[0, o : o + 1, :]
        big_sin = base_sin[0, o : o + 1, :]
        cosine = big_cos * small_cos - big_sin * small_sin
        sine = (big_sin * small_cos + big_cos * small_sin) * sign
        turned = []
        for h in range(kv_heads):
            head = keys[:, h * HEAD_WIDTH : (h + 1) * HEAD_WIDTH]
            turned.append(
                (head * cosine + pltpu.roll(head, HEAD_WIDTH // 2, 1) * sine).astype(jnp.bfloat16)
            )
        turned = jnp.concatenate(turned, axis=1)
        scores[0, o] = lax.dot_general(
            queries[o], turned, (((1,), (1,)), ((), ())), preferred_element_type=jnp.float32
        )


def fresh_scores(order, x, weight, queries, base_cos, base_sin, step_cos, step_sin):
    blocks, owners = base_cos.shape[:2]
    tokens, features = x.shape
    fresh_count = tokens // blocks
    share = fresh_count // owners
    heads = queries.shape[1]
    whole = lambda a: pl.BlockSpec(a.shape, lambda t, order: (0,) * a.ndim)
    per_block = lambda a: pl.BlockSpec((1,) + a.shape[1:], lambda t, order: (t, 0, 0))
    return pl.pallas_call(
        functools.partial(score_kernel, blocks, owners),
        grid_spec=pltpu.PrefetchScalarGridSpec(
            num_scalar_prefetch=1,
            grid=(blocks,),
            in_specs=[
                pl.BlockSpec(memory_space=pltpu.HBM),
                whole(weight),
                whole(queries),
                per_block(base_cos),
                per_block(base_sin),
                whole(step_cos),
                whole(step_sin),
            ],
            out_specs=[
                pl.BlockSpec((1, owners, heads, share), lambda t, order: (t, 0, 0, 0)),
                pl.BlockSpec((fresh_count, features), lambda t, order: (t, 0)),
            ],
            scratch_shapes=[
                pltpu.VMEM((2, fresh_count, features), jnp.bfloat16),
                pltpu.SemaphoreType.DMA((2,)),
            ],
        ),
        out_shape=[
            jax.ShapeDtypeStruct((blocks, owners, heads, share), jnp.float32),
            jax.ShapeDtypeStruct((tokens, features), jnp.bfloat16),
        ],
        compiler_params=pltpu.CompilerParams(vmem_limit_bytes=40 * 1024 * 1024),
    )(order, x, weight, queries, base_cos, base_sin, step_cos, step_sin)


def per_device(
    prefill_states,
    key_weight,
    value_weight,
    page_slot,
    decode_states,
    query_weight,
    cache_keys,
    cache_values,
    cached_length,
):
    groups = lax.axis_size("group")
    ranks = lax.axis_size("tensor")
    group = lax.axis_index("group")
    rank = lax.axis_index("tensor")
    tokens, features = prefill_states.shape
    fresh_count = tokens // ranks
    pages = fresh_count // PAGE
    kv_heads = key_weight.shape[1] // HEAD_WIDTH
    rows = decode_states.shape[0]
    share = fresh_count // groups
    span = fresh_count // rows
    senders = span // share
    assert senders * share == span
    own_row = group // senders
    offset = (group % senders) * share
    inv_scale = 1.0 / HEAD_WIDTH**0.5

    local_queries = jnp.dot(decode_states, query_weight, preferred_element_type=jnp.float32)
    local_heads = local_queries.shape[1] // HEAD_WIDTH
    heads = local_heads * ranks
    per_kv = heads // kv_heads
    local_queries = apply_rotary(
        local_queries.reshape(rows, local_heads, HEAD_WIDTH),
        (cached_length + ranks * span)[:, None],
    ).astype(jnp.bfloat16)
    every_query = lax.all_gather(
        local_queries.reshape(rows, local_heads * HEAD_WIDTH), ("group", "tensor")
    )
    every_query = every_query.reshape(groups, ranks, rows, local_heads, HEAD_WIDTH)
    every_length = lax.all_gather(cached_length, "group")
    slots = lax.all_gather(page_slot.reshape(pages), "tensor")

    index = jnp.arange(pages, dtype=jnp.int32)
    order = jnp.sum(
        jnp.where(slots[:, None, :] == index[None, :, None], index[None, None, :], 0), axis=-1
    )
    fresh_length = lax.dynamic_index_in_dim(every_length, own_row, 1, keepdims=False)
    fresh_query = lax.dynamic_index_in_dim(every_query, own_row, 2, keepdims=False)
    fresh_query = fresh_query.reshape(groups, heads, 1, HEAD_WIDTH)
    own_kv = (jnp.arange(heads) // per_kv)[:, None] == jnp.arange(kv_heads)[None, :]
    spread = jnp.where(own_kv[None, :, :, None], fresh_query, jnp.zeros_like(fresh_query))
    spread = spread.reshape(groups, heads, kv_heads * HEAD_WIDTH)
    base = (
        fresh_length[None, :] + jnp.arange(ranks, dtype=jnp.int32)[:, None] * span + offset
    )
    base_cos, base_sin = full_tables(base)
    step_cos, step_sin = full_tables(jnp.arange(share, dtype=jnp.int32))
    partial_scores, sorted_x = fresh_scores(
        order.reshape(-1), prefill_states, key_weight, spread, base_cos, base_sin, step_cos, step_sin
    )
    partial_scores = partial_scores.transpose(2, 0, 1, 3)
    scores = lax.psum_scatter(partial_scores, "tensor", scatter_dimension=0, tiled=True) * inv_scale

    grouped = lax.dynamic_index_in_dim(every_query, group, 0, keepdims=False)
    grouped = grouped.transpose(1, 0, 2, 3).reshape(rows, kv_heads, per_kv, HEAD_WIDTH)
    context_dev = cache_keys.shape[1]
    prior_keys = cache_keys.reshape(rows, context_dev, kv_heads, HEAD_WIDTH)
    prior_values = cache_values.reshape(rows, context_dev, kv_heads, HEAD_WIDTH)
    old_scores = (
        jnp.einsum("bhgd,blhd->bhgl", grouped, prior_keys, preferred_element_type=jnp.float32)
        * inv_scale
    )
    usable = (rank * context_dev + jnp.arange(context_dev, dtype=jnp.int32))[
        None, :
    ] < cached_length[:, None]
    old_scores = jnp.where(usable[:, None, None, :], old_scores, masked_score)
    old_peak = jnp.max(old_scores, axis=-1)
    old_weights = jnp.exp(old_scores - old_peak[..., None])
    old_total = jnp.sum(old_weights, axis=-1)
    old_sum = jnp.einsum(
        "bhgl,blhd->bhgd",
        old_weights.astype(jnp.bfloat16),
        prior_values,
        preferred_element_type=jnp.float32,
    )

    peak = jnp.max(scores, axis=(1, 3))
    weights = jnp.exp(scores - peak[:, None, :, None])
    total = jnp.sum(weights, axis=(1, 3))
    weights = lax.all_gather(weights.astype(jnp.bfloat16), "tensor", axis=0, tiled=True)
    mixed = jnp.einsum(
        "htos,tosf->ohf",
        weights,
        sorted_x.reshape(ranks, groups, share, features),
        preferred_element_type=jnp.float32,
    )
    fresh_sum = jnp.einsum(
        "oknf,fkd->oknd",
        mixed.astype(jnp.bfloat16).reshape(groups, kv_heads, per_kv, features),
        value_weight.reshape(features, kv_heads, HEAD_WIDTH),
        preferred_element_type=jnp.float32,
    ).reshape(groups, heads, HEAD_WIDTH)

    fresh_sum = lax.psum_scatter(fresh_sum, "tensor", scatter_dimension=1, tiled=True)
    fresh_stats = jnp.stack([peak.T, total.T], axis=-1)
    fresh_all = jnp.concatenate([fresh_sum, fresh_stats], axis=-1)
    fresh_all = lax.all_to_all(fresh_all, "group", 0, 0, tiled=True)

    old_all = jnp.concatenate(
        [
            old_sum.reshape(rows, heads, HEAD_WIDTH),
            old_peak.reshape(rows, heads, 1),
            old_total.reshape(rows, heads, 1),
        ],
        axis=-1,
    )
    old_all = lax.all_to_all(
        old_all.reshape(rows, ranks, local_heads, HEAD_WIDTH + 2).transpose(1, 0, 2, 3),
        "tensor", 0, 0, tiled=True,
    )
    fresh_all = fresh_all.reshape(rows, senders, local_heads, HEAD_WIDTH + 2).transpose(1, 0, 2, 3)
    parts = jnp.concatenate([old_all, fresh_all], axis=0)
    peaks = parts[..., HEAD_WIDTH]
    factor = jnp.exp(peaks - jnp.max(peaks, axis=0))
    numerator = jnp.sum(parts[..., :HEAD_WIDTH] * factor[..., None], axis=0)
    denominator = jnp.sum(parts[..., HEAD_WIDTH + 1] * factor, axis=0)
    result = numerator / denominator[..., None]
    return result.reshape(rows, local_heads * HEAD_WIDTH).astype(jnp.bfloat16)


def solution(mesh):
    placed = (
        P("group", "tensor"),
        P("tensor", None),
        P("tensor", None),
        P("group", "tensor", None),
        P("group", None),
        P(None, "tensor"),
        P("group", "tensor", None),
        P("group", "tensor", None),
        P("group"),
    )
    return jax.shard_map(
        per_device, mesh=mesh, in_specs=placed, out_specs=P("group", "tensor"), check_vma=False
    )
```

```python
import functools

import jax
import jax.numpy as jnp
from jax import lax
from jax.experimental import pallas as pl
from jax.experimental.pallas import tpu as pltpu
from jax.sharding import PartitionSpec as P

HEAD_WIDTH = 128
PAGE = 8


rope_theta = 500000.0
masked_score = -1e30


def angles_of(positions):
    half_width = HEAD_WIDTH // 2
    index_float = jnp.arange(half_width, dtype=jnp.float32)
    frequency = rope_theta ** (-2.0 * index_float / HEAD_WIDTH)
    return positions[..., None].astype(jnp.float32) * frequency


def full_tables(positions):
    angles = angles_of(positions)
    cosine_part = jnp.cos(angles)
    sine_part = jnp.sin(angles)
    return (
        jnp.concatenate([cosine_part, cosine_part], axis=-1),
        jnp.concatenate([sine_part, sine_part], axis=-1),
    )


def apply_rotary(vectors, positions):
    half_width = vectors.shape[-1] // 2
    angles = angles_of(positions)
    cosine_part = jnp.cos(angles)
    sine_part = jnp.sin(angles)
    first_half = vectors[..., :half_width]
    second_half = vectors[..., half_width:]
    return jnp.concatenate(
        [
            first_half * cosine_part - second_half * sine_part,
            second_half * cosine_part + first_half * sine_part,
        ],
        axis=-1,
    )


def score_kernel(
    blocks, owners, order, x_ref, weight, queries, base_cos, base_sin, step_cos, step_sin,
    scores, sorted_x, held, sems,
):
    block = pl.program_id(0)
    fresh_count = held.shape[1]
    pages = fresh_count // PAGE
    share = fresh_count // owners
    kv_heads = weight.shape[1] // HEAD_WIDTH

    def fetch(which, slot):
        def one(s, carry):
            page = order[which * pages + s]
            start = pl.multiple_of(which * fresh_count + page * PAGE, PAGE)
            pltpu.make_async_copy(
                x_ref.at[pl.ds(start, PAGE), :],
                held.at[slot, pl.ds(pl.multiple_of(s * PAGE, PAGE), PAGE), :],
                sems.at[slot],
            ).start()
            return carry

        lax.fori_loop(0, pages, one, 0, unroll=8)

    slot = lax.rem(block, 2)

    @pl.when(block == 0)
    def _():
        fetch(0, 0)

    @pl.when(block + 1 < blocks)
    def _():
        fetch(block + 1, 1 - slot)

    pltpu.make_async_copy(x_ref.at[pl.ds(0, fresh_count), :], held.at[slot], sems.at[slot]).wait()
    x = held[slot]
    sorted_x[...] = x
    lane = lax.broadcasted_iota(jnp.int32, (share, HEAD_WIDTH), 1)
    sign = jnp.where(lane < HEAD_WIDTH // 2, -1.0, 1.0).astype(jnp.float32)
    small_cos, small_sin = step_cos[...], step_sin[...]
    for o in range(owners):
        rows = slice(o * share, (o + 1) * share)
        keys = jnp.dot(x[rows], weight[...], preferred_element_type=jnp.float32)
        big_cos = base_cos[0, o : o + 1, :]
        big_sin = base_sin[0, o : o + 1, :]
        cosine = big_cos * small_cos - big_sin * small_sin
        sine = (big_sin * small_cos + big_cos * small_sin) * sign
        turned = []
        for h in range(kv_heads):
            head = keys[:, h * HEAD_WIDTH : (h + 1) * HEAD_WIDTH]
            turned.append(
                (head * cosine + pltpu.roll(head, HEAD_WIDTH // 2, 1) * sine).astype(jnp.bfloat16)
            )
        turned = jnp.concatenate(turned, axis=1)
        found = lax.dot_general(
            queries[o], turned, (((1,), (1,)), ((), ())), preferred_element_type=jnp.float32
        )
        local_heads = scores.shape[3]
        for j in range(scores.shape[0]):
            scores[j, 0, o] = found[j * local_heads : (j + 1) * local_heads]


def fresh_scores(order, x, weight, queries, base_cos, base_sin, step_cos, step_sin):
    blocks, owners = base_cos.shape[:2]
    tokens, features = x.shape
    fresh_count = tokens // blocks
    share = fresh_count // owners
    heads = queries.shape[1]
    whole = lambda a: pl.BlockSpec(a.shape, lambda t, order: (0,) * a.ndim)
    per_block = lambda a: pl.BlockSpec((1,) + a.shape[1:], lambda t, order: (t, 0, 0))
    return pl.pallas_call(
        functools.partial(score_kernel, blocks, owners),
        grid_spec=pltpu.PrefetchScalarGridSpec(
            num_scalar_prefetch=1,
            grid=(blocks,),
            in_specs=[
                pl.BlockSpec(memory_space=pltpu.HBM),
                whole(weight),
                whole(queries),
                per_block(base_cos),
                per_block(base_sin),
                whole(step_cos),
                whole(step_sin),
            ],
            out_specs=[
                pl.BlockSpec(
                    (blocks, 1, owners, heads // blocks, share), lambda t, order: (0, t, 0, 0, 0)
                ),
                pl.BlockSpec((fresh_count, features), lambda t, order: (t, 0)),
            ],
            scratch_shapes=[
                pltpu.VMEM((2, fresh_count, features), jnp.bfloat16),
                pltpu.SemaphoreType.DMA((2,)),
            ],
        ),
        out_shape=[
            jax.ShapeDtypeStruct((blocks, blocks, owners, heads // blocks, share), jnp.float32),
            jax.ShapeDtypeStruct((tokens, features), jnp.bfloat16),
        ],
        compiler_params=pltpu.CompilerParams(vmem_limit_bytes=40 * 1024 * 1024),
    )(order, x, weight, queries, base_cos, base_sin, step_cos, step_sin)


def remote(src, dst, send_sem, recv_sem, group, rank):
    return pltpu.make_async_remote_copy(
        src_ref=src,
        dst_ref=dst,
        send_sem=send_sem,
        recv_sem=recv_sem,
        device_id={"group": group, "tensor": rank},
        device_id_type=pl.DeviceIdType.MESH,
    )


def greet_all(groups, ranks, group, rank):
    barrier = pltpu.get_barrier_semaphore()
    count = groups * ranks
    own = group * ranks + rank

    def greet(step, carry):
        peer = lax.rem(own + step, count)
        pl.semaphore_signal(
            barrier,
            inc=1,
            device_id={"group": peer // ranks, "tensor": lax.rem(peer, ranks)},
            device_id_type=pl.DeviceIdType.MESH,
        )
        return carry

    lax.fori_loop(1, count, greet, 0)
    pl.semaphore_wait(barrier, count - 1)


def gather_kernel(
    groups, ranks, senders, query, meta, own_query, fresh_query, meta_ranks, meta_groups,
    send_query, send_fresh, send_ranks, send_groups, got_query, got_fresh, got_ranks, got_groups,
):
    group, rank = lax.axis_index("group"), lax.axis_index("tensor")
    greet_all(groups, ranks, group, rank)

    def to_rank(step):
        peer = lax.rem(rank + step, ranks)
        return (
            remote(
                meta, meta_ranks.at[rank], send_ranks.at[step], got_ranks.at[rank], group, peer
            ),
            remote(
                query, own_query.at[rank], send_query.at[step], got_query.at[rank], group, peer
            ),
        )

    def to_group(step):
        peer = lax.rem(group + step, groups)
        return remote(
            meta, meta_groups.at[group], send_groups.at[step], got_groups.at[group], peer, rank
        )

    def to_fresh(step):
        peer_group = lax.rem(group + 1 + step // ranks, groups)
        peer_rank = lax.rem(rank + step, ranks)
        return remote(
            query.at[peer_group // senders],
            fresh_query.at[group, rank],
            send_fresh.at[step],
            got_fresh.at[group, rank],
            peer_group,
            peer_rank,
        )

    for step in range(1, ranks):
        for copy in to_rank(step):
            copy.start()
    for step in range(1, groups):
        to_group(step).start()

    def start(step, carry):
        to_fresh(step).start()
        return carry

    lax.fori_loop(0, (groups - 1) * ranks, start, 0)
    own_query[rank] = query[...]
    meta_ranks[rank] = meta[...]
    meta_groups[group] = meta[...]
    for step in range(1, ranks):
        source = lax.rem(rank + step, ranks)
        remote(
            query, own_query.at[source], send_query.at[step], got_query.at[source], group, source
        ).wait_recv()
        remote(
            meta, meta_ranks.at[source], send_ranks.at[step], got_ranks.at[source], group, source
        ).wait_recv()
    for step in range(1, groups):
        source = lax.rem(group + step, groups)
        remote(
            meta, meta_groups.at[source], send_groups.at[step], got_groups.at[source], source, rank
        ).wait_recv()
    for t in range(ranks):
        fresh_query[group, t] = own_query[t, group // senders]

    def finish(step, carry):
        source_group = lax.rem(group + 1 + step // ranks, groups)
        source_rank = lax.rem(rank + step, ranks)
        remote(
            query.at[0],
            fresh_query.at[source_group, source_rank],
            send_fresh.at[step],
            got_fresh.at[source_group, source_rank],
            source_group,
            source_rank,
        ).wait_recv()
        to_fresh(step).wait_send()
        return carry

    lax.fori_loop(0, (groups - 1) * ranks, finish, 0)
    for step in range(1, ranks):
        for copy in to_rank(step):
            copy.wait_send()
    for step in range(1, groups):
        to_group(step).wait_send()


def gather_queries(groups, ranks, senders, query, meta):
    rows, local_heads, width = query.shape
    dma = pltpu.SemaphoreType.DMA
    others = (groups - 1) * ranks
    vmem = pl.BlockSpec(memory_space=pltpu.VMEM)
    return pl.pallas_call(
        functools.partial(gather_kernel, groups, ranks, senders),
        in_specs=[vmem] * 2,
        out_specs=[vmem] * 4,
        out_shape=[
            jax.ShapeDtypeStruct((ranks, rows, local_heads, width), query.dtype),
            jax.ShapeDtypeStruct((groups, ranks, local_heads, width), query.dtype),
            jax.ShapeDtypeStruct((ranks,) + meta.shape, meta.dtype),
            jax.ShapeDtypeStruct((groups,) + meta.shape, meta.dtype),
        ],
        scratch_shapes=[
            dma((ranks,)), dma((others,)), dma((ranks,)), dma((groups,)),
            dma((ranks,)), dma((groups, ranks)), dma((ranks,)), dma((groups,)),
        ],
        compiler_params=pltpu.CompilerParams(collective_id=0, has_side_effects=True),
    )(query, meta)


def weight_kernel(
    ranks, scale, partial_scores, weights, stats, paired, chip_sums, incoming,
    send_pair, send_sum, send_weight, send_on, got_pair, got_sum, got_weight,
):
    group, rank = lax.axis_index("group"), lax.axis_index("tensor")
    chips = ranks // 2
    core, chip = lax.rem(rank, 2), rank // 2
    partner = chip * 2 + 1 - core
    barrier = pltpu.get_barrier_semaphore()

    def peer_of(step):
        other = lax.rem(chip + step, chips)
        return other, other * 2 + core

    for peer in [partner] + [peer_of(step)[1] for step in range(1, chips)]:
        pl.semaphore_signal(
            barrier,
            inc=1,
            device_id={"group": group, "tensor": peer},
            device_id_type=pl.DeviceIdType.MESH,
        )
    pl.semaphore_wait(barrier, chips)

    order = list(range(1, chips)) + [0]

    def pair_copy(step):
        other = lax.rem(chip + step, chips)
        return remote(
            partial_scores.at[other * 2 + 1 - core],
            paired.at[other],
            send_pair.at[other],
            got_pair.at[other],
            group,
            partner,
        )

    def sum_copy(step):
        other, peer = peer_of(step)
        return remote(
            chip_sums.at[other], incoming.at[chip], send_sum.at[step], got_sum.at[chip], group, peer
        )

    for step in order:
        pair_copy(step).start()
    for step in order:
        other, peer = peer_of(step)
        pair_copy(step).wait_recv()
        chip_sums[other] = partial_scores[peer] + paired[other]
        if step:
            sum_copy(step).start()
    total = chip_sums[chip]
    for step in range(1, chips):
        other, peer = peer_of(step)
        remote(
            chip_sums.at[other], incoming.at[other], send_sum.at[step], got_sum.at[other], group, peer
        ).wait_recv()
        total = total + incoming[other]
    total = total * scale
    peak = jnp.max(jnp.max(total, axis=0), axis=-1, keepdims=True)
    exact = jnp.exp(total - peak[None])
    weights[rank] = exact.astype(jnp.bfloat16)

    def weight_copy(step):
        other, peer = peer_of(step)
        return remote(
            weights.at[rank], weights.at[rank], send_weight.at[step], got_weight.at[rank], group, peer
        )

    def on_copy(step):
        other, peer = peer_of(step)
        return remote(
            weights.at[peer], weights.at[peer], send_on.at[step], got_weight.at[peer], group, partner
        )

    for step in range(1, chips):
        weight_copy(step).start()
    on_copy(0).start()
    amount = jnp.sum(jnp.sum(exact, axis=0), axis=-1, keepdims=True)
    lane = lax.broadcasted_iota(jnp.int32, stats.shape, 2)
    stats[...] = jnp.where(lane == 0, peak, jnp.where(lane == 1, amount, 0.0))
    for step in range(1, chips):
        other, peer = peer_of(step)
        remote(
            weights.at[peer], weights.at[peer], send_weight.at[step], got_weight.at[peer], group, peer
        ).wait_recv()
        on_copy(step).start()
    for step in range(chips):
        other = lax.rem(chip + step, chips) * 2 + 1 - core
        remote(
            weights.at[other], weights.at[other], send_on.at[step], got_weight.at[other], group, partner
        ).wait_recv()
    for step in range(chips):
        pair_copy(step).wait_send()
        on_copy(step).wait_send()
        if step:
            sum_copy(step).wait_send()
            weight_copy(step).wait_send()


def fresh_weights(partial_scores, scale):
    ranks, blocks, owners, local_heads, share = partial_scores.shape
    chips = ranks // 2
    dma = pltpu.SemaphoreType.DMA
    vmem = pl.BlockSpec(memory_space=pltpu.VMEM)
    held = pltpu.VMEM((chips, blocks, owners, local_heads, share), jnp.float32)
    return pl.pallas_call(
        functools.partial(weight_kernel, ranks, scale),
        in_specs=[vmem],
        out_specs=[vmem] * 2,
        out_shape=[
            jax.ShapeDtypeStruct(partial_scores.shape, jnp.bfloat16),
            jax.ShapeDtypeStruct((owners, local_heads, HEAD_WIDTH), jnp.float32),
        ],
        scratch_shapes=[held] * 3 + [dma((chips,))] * 6 + [dma((ranks,))],
        compiler_params=pltpu.CompilerParams(
            collective_id=1, has_side_effects=True, vmem_limit_bytes=32 * 1024 * 1024
        ),
    )(partial_scores)


def blend_kernel(
    groups, ranks, senders, fresh, stats, old, out, fresh_in, stats_in, old_in,
    send_fresh, send_stats, send_old, got_fresh, got_stats, got_old,
):
    group, rank = lax.axis_index("group"), lax.axis_index("tensor")
    rows = out.shape[0]
    count = groups * ranks
    own = group * ranks + rank
    greet_all(groups, ranks, group, rank)

    def peer_of(step):
        peer = lax.rem(own + step, count)
        return peer // ranks, lax.rem(peer, ranks)

    def fresh_copy(step):
        peer_group, peer_rank = peer_of(step)
        return remote(
            fresh.at[peer_group, peer_rank],
            fresh_in.at[group, rank],
            send_fresh.at[step],
            got_fresh.at[group, rank],
            peer_group,
            peer_rank,
        )

    def stats_copy(step):
        peer = lax.rem(group + step, groups)
        return remote(
            stats.at[peer], stats_in.at[group], send_stats.at[step], got_stats.at[group], peer, rank
        )

    def old_copy(step):
        peer = lax.rem(rank + step, ranks)
        return remote(
            old.at[peer], old_in.at[rank], send_old.at[step], got_old.at[rank], group, peer
        )

    for step in range(1, ranks):
        old_copy(step).start()
    for step in range(1, groups):
        stats_copy(step).start()

    def start(step, carry):
        fresh_copy(step).start()
        return carry

    lax.fori_loop(1, count, start, 0)
    old_in[rank] = old[rank]
    stats_in[group] = stats[group]
    fresh_in[group, rank] = fresh[group, rank]
    for step in range(1, ranks):
        source = lax.rem(rank + step, ranks)
        remote(
            old.at[source], old_in.at[source], send_old.at[step], got_old.at[source], group, source
        ).wait_recv()
    for step in range(1, groups):
        source = lax.rem(group + step, groups)
        remote(
            stats.at[source], stats_in.at[source], send_stats.at[step], got_stats.at[source], source, rank
        ).wait_recv()

    def finish(step, carry):
        source_group, source_rank = peer_of(step)
        remote(
            fresh.at[source_group, source_rank],
            fresh_in.at[source_group, source_rank],
            send_fresh.at[step],
            got_fresh.at[source_group, source_rank],
            source_group,
            source_rank,
        ).wait_recv()
        fresh_copy(step).wait_send()
        return carry

    lax.fori_loop(1, count, finish, 0)
    for row in range(rows):
        peaks, totals, sums = [], [], []
        for t in range(ranks):
            about = old_in[t, rows]
            peaks.append(about[:, row : row + 1])
            totals.append(about[:, rows + row : rows + row + 1])
            sums.append(old_in[t, row])
        for sender in range(row * senders, (row + 1) * senders):
            about = stats_in[sender]
            peaks.append(about[:, 0:1])
            totals.append(about[:, 1:2])
            sums.append(jnp.sum(fresh_in[sender], axis=0))
        top = functools.reduce(jnp.maximum, peaks)
        factors = [jnp.exp(peak - top) for peak in peaks]
        numerator = sum(a * b for a, b in zip(sums, factors))
        denominator = sum(a * b for a, b in zip(totals, factors))
        out[row] = (numerator / denominator).astype(out.dtype)
    for step in range(1, ranks):
        old_copy(step).wait_send()
    for step in range(1, groups):
        stats_copy(step).wait_send()


def blend(senders, fresh, stats, old):
    groups, ranks, local_heads, width = fresh.shape
    rows = old.shape[1] - 1
    dma = pltpu.SemaphoreType.DMA
    vmem = pl.BlockSpec(memory_space=pltpu.VMEM)
    return pl.pallas_call(
        functools.partial(blend_kernel, groups, ranks, senders),
        in_specs=[vmem] * 3,
        out_specs=vmem,
        out_shape=jax.ShapeDtypeStruct((rows, local_heads, width), jnp.bfloat16),
        scratch_shapes=[
            pltpu.VMEM(fresh.shape, jnp.float32),
            pltpu.VMEM(stats.shape, jnp.float32),
            pltpu.VMEM(old.shape, jnp.float32),
            dma((groups * ranks,)), dma((groups,)), dma((ranks,)),
            dma((groups, ranks)), dma((groups,)), dma((ranks,)),
        ],
        compiler_params=pltpu.CompilerParams(collective_id=2, has_side_effects=True),
    )(fresh, stats, old)


def per_device(
    prefill_states,
    key_weight,
    value_weight,
    page_slot,
    decode_states,
    query_weight,
    cache_keys,
    cache_values,
    cached_length,
):
    groups = lax.axis_size("group")
    ranks = lax.axis_size("tensor")
    group = lax.axis_index("group")
    rank = lax.axis_index("tensor")
    tokens, features = prefill_states.shape
    fresh_count = tokens // ranks
    pages = fresh_count // PAGE
    kv_heads = key_weight.shape[1] // HEAD_WIDTH
    rows = decode_states.shape[0]
    share = fresh_count // groups
    span = fresh_count // rows
    senders = span // share
    assert senders * share == span
    own_row = group // senders
    offset = (group % senders) * share
    inv_scale = 1.0 / HEAD_WIDTH**0.5

    local_queries = jnp.dot(decode_states, query_weight, preferred_element_type=jnp.float32)
    local_heads = local_queries.shape[1] // HEAD_WIDTH
    heads = local_heads * ranks
    per_kv = heads // kv_heads
    local_queries = apply_rotary(
        local_queries.reshape(rows, local_heads, HEAD_WIDTH),
        (cached_length + ranks * span)[:, None],
    ).astype(jnp.bfloat16)
    pad = jnp.zeros((1, HEAD_WIDTH), jnp.int32)
    meta = jnp.concatenate(
        [
            pad.at[0, :pages].set(page_slot.reshape(pages)),
            pad.at[0, :rows].set(cached_length),
            jnp.zeros((6, HEAD_WIDTH), jnp.int32),
        ],
        axis=0,
    )
    own_query, fresh_query, meta_ranks, meta_groups = gather_queries(
        groups, ranks, senders, local_queries, meta
    )
    slots = meta_ranks[:, 0, :pages]
    every_length = meta_groups[:, 1, :rows]

    index = jnp.arange(pages, dtype=jnp.int32)
    order = jnp.sum(
        jnp.where(slots[:, None, :] == index[None, :, None], index[None, None, :], 0), axis=-1
    )
    fresh_length = lax.dynamic_index_in_dim(every_length, own_row, 1, keepdims=False)
    fresh_query = fresh_query.reshape(groups, heads, 1, HEAD_WIDTH)
    own_kv = (jnp.arange(heads) // per_kv)[:, None] == jnp.arange(kv_heads)[None, :]
    spread = jnp.where(own_kv[None, :, :, None], fresh_query, jnp.zeros_like(fresh_query))
    spread = spread.reshape(groups, heads, kv_heads * HEAD_WIDTH)
    base = (
        fresh_length[None, :] + jnp.arange(ranks, dtype=jnp.int32)[:, None] * span + offset
    )
    base_cos, base_sin = full_tables(base)
    step_cos, step_sin = full_tables(jnp.arange(share, dtype=jnp.int32))
    partial_scores, sorted_x = fresh_scores(
        order.reshape(-1), prefill_states, key_weight, spread, base_cos, base_sin, step_cos, step_sin
    )
    weights, fresh_stats = fresh_weights(partial_scores, inv_scale)

    grouped = own_query.transpose(1, 0, 2, 3).reshape(rows, kv_heads, per_kv, HEAD_WIDTH)
    context_dev = cache_keys.shape[1]
    prior_keys = cache_keys.reshape(rows, context_dev, kv_heads, HEAD_WIDTH)
    prior_values = cache_values.reshape(rows, context_dev, kv_heads, HEAD_WIDTH)
    old_scores = (
        jnp.einsum("bhgd,blhd->bhgl", grouped, prior_keys, preferred_element_type=jnp.float32)
        * inv_scale
    )
    usable = (rank * context_dev + jnp.arange(context_dev, dtype=jnp.int32))[
        None, :
    ] < cached_length[:, None]
    old_scores = jnp.where(usable[:, None, None, :], old_scores, masked_score)
    old_peak = jnp.max(old_scores, axis=-1)
    old_weights = jnp.exp(old_scores - old_peak[..., None])
    old_total = jnp.sum(old_weights, axis=-1)
    old_sum = jnp.einsum(
        "bhgl,blhd->bhgd",
        old_weights.astype(jnp.bfloat16),
        prior_values,
        preferred_element_type=jnp.float32,
    )

    mixed = jnp.einsum(
        "jtois,tosf->ojif",
        weights,
        sorted_x.reshape(ranks, groups, share, features),
        preferred_element_type=jnp.float32,
    )
    fresh_sum = jnp.einsum(
        "oknf,fkd->oknd",
        mixed.astype(jnp.bfloat16).reshape(groups, kv_heads, per_kv, features),
        value_weight.reshape(features, kv_heads, HEAD_WIDTH),
        preferred_element_type=jnp.float32,
    ).reshape(groups, ranks, local_heads, HEAD_WIDTH)

    about = jnp.concatenate(
        [old_peak.reshape(rows, heads), old_total.reshape(rows, heads)], axis=0
    )
    about = jnp.pad(about.T, ((0, 0), (0, HEAD_WIDTH - 2 * rows)))
    old_all = jnp.concatenate(
        [
            old_sum.reshape(rows, ranks, local_heads, HEAD_WIDTH).transpose(1, 0, 2, 3),
            about.reshape(ranks, 1, local_heads, HEAD_WIDTH),
        ],
        axis=1,
    )
    result = blend(senders, fresh_sum, fresh_stats, old_all)
    return result.reshape(rows, local_heads * HEAD_WIDTH)


def solution(mesh):
    placed = (
        P("group", "tensor"),
        P("tensor", None),
        P("tensor", None),
        P("group", "tensor", None),
        P("group", None),
        P(None, "tensor"),
        P("group", "tensor", None),
        P("group", "tensor", None),
        P("group"),
    )
    return jax.shard_map(
        per_device, mesh=mesh, in_specs=placed, out_specs=P("group", "tensor"), check_vma=False
    )
```

```python
import functools

import jax
import jax.numpy as jnp
from jax import lax
from jax.experimental import pallas as pl
from jax.experimental.pallas import tpu as pltpu
from jax.sharding import PartitionSpec as P

HEAD_WIDTH = 128
PAGE = 8


rope_theta = 500000.0
masked_score = -1e30


def angles_of(positions):
    half_width = HEAD_WIDTH // 2
    index_float = jnp.arange(half_width, dtype=jnp.float32)
    frequency = rope_theta ** (-2.0 * index_float / HEAD_WIDTH)
    return positions[..., None].astype(jnp.float32) * frequency


def full_tables(positions):
    angles = angles_of(positions)
    cosine_part = jnp.cos(angles)
    sine_part = jnp.sin(angles)
    return (
        jnp.concatenate([cosine_part, cosine_part], axis=-1),
        jnp.concatenate([sine_part, sine_part], axis=-1),
    )


def apply_rotary(vectors, positions):
    half_width = vectors.shape[-1] // 2
    angles = angles_of(positions)
    cosine_part = jnp.cos(angles)
    sine_part = jnp.sin(angles)
    first_half = vectors[..., :half_width]
    second_half = vectors[..., half_width:]
    return jnp.concatenate(
        [
            first_half * cosine_part - second_half * sine_part,
            second_half * cosine_part + first_half * sine_part,
        ],
        axis=-1,
    )


def remote(src, dst, send_sem, recv_sem, group, rank):
    return pltpu.make_async_remote_copy(
        src_ref=src,
        dst_ref=dst,
        send_sem=send_sem,
        recv_sem=recv_sem,
        device_id={"group": group, "tensor": rank},
        device_id_type=pl.DeviceIdType.MESH,
    )


def greet_all(groups, ranks, group, rank):
    barrier = pltpu.get_barrier_semaphore()
    count = groups * ranks
    own = group * ranks + rank

    def greet(step, carry):
        peer = lax.rem(own + step, count)
        pl.semaphore_signal(
            barrier,
            inc=1,
            device_id={"group": peer // ranks, "tensor": lax.rem(peer, ranks)},
            device_id_type=pl.DeviceIdType.MESH,
        )
        return carry

    lax.fori_loop(1, count, greet, 0)
    pl.semaphore_wait(barrier, count - 1)


def gather_kernel(
    groups, ranks, senders, query, meta, states, weight,
    own_query, fresh_query, meta_ranks, meta_groups, keys,
    send_query, send_fresh, send_ranks, send_groups, got_query, got_fresh, got_ranks, got_groups,
    state_tiles, key_tiles, state_sems, key_sems,
):
    group, rank = lax.axis_index("group"), lax.axis_index("tensor")
    tile = state_tiles.shape[1]
    tiles = states.shape[0] // tile

    def state_copy(step, slot):
        start = pl.multiple_of(step * tile, tile)
        return pltpu.make_async_copy(
            states.at[pl.ds(start, tile), :], state_tiles.at[slot], state_sems.at[slot]
        )

    def key_copy(step, slot):
        start = pl.multiple_of(step * tile, tile)
        return pltpu.make_async_copy(
            key_tiles.at[slot], keys.at[pl.ds(start, tile), :], key_sems.at[slot]
        )

    state_copy(0, 0).start()
    greet_all(groups, ranks, group, rank)

    def to_rank(step):
        peer = lax.rem(rank + step, ranks)
        return (
            remote(
                meta, meta_ranks.at[rank], send_ranks.at[step], got_ranks.at[rank], group, peer
            ),
            remote(
                query, own_query.at[rank], send_query.at[step], got_query.at[rank], group, peer
            ),
        )

    def to_group(step):
        peer = lax.rem(group + step, groups)
        return remote(
            meta, meta_groups.at[group], send_groups.at[step], got_groups.at[group], peer, rank
        )

    def to_fresh(step):
        peer_group = lax.rem(group + 1 + step // ranks, groups)
        peer_rank = lax.rem(rank + step, ranks)
        return remote(
            query.at[peer_group // senders],
            fresh_query.at[group, rank],
            send_fresh.at[step],
            got_fresh.at[group, rank],
            peer_group,
            peer_rank,
        )

    for step in range(1, ranks):
        for copy in to_rank(step):
            copy.start()
    for step in range(1, groups):
        to_group(step).start()

    def start(step, carry):
        to_fresh(step).start()
        return carry

    lax.fori_loop(0, (groups - 1) * ranks, start, 0)
    own_query[rank] = query[...]
    meta_ranks[rank] = meta[...]
    meta_groups[group] = meta[...]

    def project(step, carry):
        slot = lax.rem(step, 2)

        @pl.when(step + 1 < tiles)
        def _():
            state_copy(step + 1, 1 - slot).start()

        state_copy(step, slot).wait()

        @pl.when(step >= 2)
        def _():
            key_copy(step - 2, slot).wait()

        key_tiles[slot] = jnp.dot(
            state_tiles[slot], weight[...], preferred_element_type=jnp.float32
        ).astype(jnp.bfloat16)
        key_copy(step, slot).start()
        return carry

    lax.fori_loop(0, tiles, project, 0)
    key_copy(tiles - 2, (tiles - 2) % 2).wait()
    key_copy(tiles - 1, (tiles - 1) % 2).wait()
    for step in range(1, ranks):
        source = lax.rem(rank + step, ranks)
        remote(
            query, own_query.at[source], send_query.at[step], got_query.at[source], group, source
        ).wait_recv()
        remote(
            meta, meta_ranks.at[source], send_ranks.at[step], got_ranks.at[source], group, source
        ).wait_recv()
    for step in range(1, groups):
        source = lax.rem(group + step, groups)
        remote(
            meta, meta_groups.at[source], send_groups.at[step], got_groups.at[source], source, rank
        ).wait_recv()
    for t in range(ranks):
        fresh_query[group, t] = own_query[t, group // senders]

    def finish(step, carry):
        source_group = lax.rem(group + 1 + step // ranks, groups)
        source_rank = lax.rem(rank + step, ranks)
        remote(
            query.at[0],
            fresh_query.at[source_group, source_rank],
            send_fresh.at[step],
            got_fresh.at[source_group, source_rank],
            source_group,
            source_rank,
        ).wait_recv()
        to_fresh(step).wait_send()
        return carry

    lax.fori_loop(0, (groups - 1) * ranks, finish, 0)
    for step in range(1, ranks):
        for copy in to_rank(step):
            copy.wait_send()
    for step in range(1, groups):
        to_group(step).wait_send()


def gather_queries(groups, ranks, senders, query, meta, states, weight):
    rows, local_heads, width = query.shape
    dma = pltpu.SemaphoreType.DMA
    others = (groups - 1) * ranks
    tokens, features = states.shape
    tile = tokens // ranks
    hbm = pl.BlockSpec(memory_space=pltpu.HBM)
    vmem = pl.BlockSpec(memory_space=pltpu.VMEM)
    return pl.pallas_call(
        functools.partial(gather_kernel, groups, ranks, senders),
        in_specs=[vmem, vmem, hbm, vmem],
        out_specs=[vmem] * 4 + [hbm],
        out_shape=[
            jax.ShapeDtypeStruct((ranks, rows, local_heads, width), query.dtype),
            jax.ShapeDtypeStruct((groups, ranks, local_heads, width), query.dtype),
            jax.ShapeDtypeStruct((ranks,) + meta.shape, meta.dtype),
            jax.ShapeDtypeStruct((groups,) + meta.shape, meta.dtype),
            jax.ShapeDtypeStruct((tokens, weight.shape[1]), jnp.bfloat16),
        ],
        scratch_shapes=[
            dma((ranks,)), dma((others,)), dma((ranks,)), dma((groups,)),
            dma((ranks,)), dma((groups, ranks)), dma((ranks,)), dma((groups,)),
            pltpu.VMEM((2, tile, features), jnp.bfloat16),
            pltpu.VMEM((2, tile, weight.shape[1]), jnp.bfloat16),
            dma((2,)), dma((2,)),
        ],
        compiler_params=pltpu.CompilerParams(
            collective_id=0, has_side_effects=True, vmem_limit_bytes=32 * 1024 * 1024
        ),
    )(query, meta, states, weight)


def weight_kernel(
    ranks, owners, scale, keys, queries, base_cos, base_sin, step_cos, step_sin, owner_of,
    cache_keys, cache_values, own_queries, limits,
    weights, stats, old,
    partial_scores, paired, chip_sums, incoming, key_tiles, turned, old_keys, old_values,
    send_pair, send_sum, send_weight, send_on, got_pair, got_sum, got_weight, key_sems, old_sems,
):
    group, rank = lax.axis_index("group"), lax.axis_index("tensor")
    chips = ranks // 2
    core, chip = lax.rem(rank, 2), rank // 2
    partner = chip * 2 + 1 - core
    tile = turned.shape[0]
    local_heads = weights.shape[2]
    heads = local_heads * ranks
    kv_heads = turned.shape[1] // HEAD_WIDTH
    per_kv = heads // kv_heads
    rows, context_dev = cache_keys.shape[:2]
    pages = tile // PAGE

    def key_copy(step, slot):
        start = pl.multiple_of(step * tile, tile)
        return pltpu.make_async_copy(
            keys.at[pl.ds(start, tile), :], key_tiles.at[slot], key_sems.at[slot]
        )

    key_copy(0, 0).start()
    barrier = pltpu.get_barrier_semaphore()

    def peer_of(step):
        other = lax.rem(chip + step, chips)
        return other, other * 2 + core

    for peer in [partner] + [peer_of(step)[1] for step in range(1, chips)]:
        pl.semaphore_signal(
            barrier,
            inc=1,
            device_id={"group": group, "tensor": peer},
            device_id_type=pl.DeviceIdType.MESH,
        )
    key_old = pltpu.make_async_copy(cache_keys, old_keys, old_sems.at[0])
    value_old = pltpu.make_async_copy(cache_values, old_values, old_sems.at[1])
    pl.semaphore_wait(barrier, chips)

    def pair_copy(block):
        return remote(
            partial_scores.at[1 - core, block],
            paired.at[block],
            send_pair.at[block],
            got_pair.at[block],
            group,
            partner,
        )

    def sum_copy(step, block):
        other, peer = peer_of(step)
        return remote(
            chip_sums.at[other, block],
            incoming.at[chip, block],
            send_sum.at[step, block],
            got_sum.at[chip, block],
            group,
            peer,
        )

    def add_pair(block):
        pair_copy(block).wait_recv()
        for step in range(1, chips):
            other, peer = peer_of(step)
            chip_sums[other, block] = partial_scores[core, block, other] + paired[block, other]
            sum_copy(step, block).start()
        chip_sums[chip, block] = partial_scores[core, block, chip] + paired[block, chip]

    lane = lax.broadcasted_iota(jnp.int32, (1, HEAD_WIDTH), 1)
    sign = jnp.where(lane < HEAD_WIDTH // 2, -1.0, 1.0).astype(jnp.float32)

    def score(block, carry):
        slot = lax.rem(block, 2)

        @pl.when(block + 1 < ranks)
        def _():
            key_copy(block + 1, 1 - slot).start()

        key_copy(block, slot).wait()
        span = pl.ds(pl.multiple_of(block * pages, pages), pages)
        big_cos = base_cos[span, :].reshape(pages, 1, HEAD_WIDTH)
        big_sin = base_sin[span, :].reshape(pages, 1, HEAD_WIDTH)
        small_cos = step_cos[...].reshape(1, PAGE, HEAD_WIDTH)
        small_sin = step_sin[...].reshape(1, PAGE, HEAD_WIDTH)
        cosine = (big_cos * small_cos - big_sin * small_sin).reshape(tile, HEAD_WIDTH)
        sine = (big_sin * small_cos + big_cos * small_sin).reshape(tile, HEAD_WIDTH) * sign
        for h in range(kv_heads):
            columns = slice(h * HEAD_WIDTH, (h + 1) * HEAD_WIDTH)
            head = key_tiles[slot, :, columns].astype(jnp.float32)
            turned[:, columns] = (
                head * cosine + pltpu.roll(head, HEAD_WIDTH // 2, 1) * sine
            ).astype(jnp.bfloat16)
        found = lax.dot_general(
            queries[...], turned[...], (((1,), (1,)), ((), ())), preferred_element_type=jnp.float32
        )
        owner = owner_of[block]
        kept = jnp.zeros((heads, tile), jnp.float32)
        for o in range(owners):
            kept = jnp.where(owner == o, found[o * heads : (o + 1) * heads], kept)
        for j in range(ranks):
            partial_scores[j % 2, block, j // 2] = kept[j * local_heads : (j + 1) * local_heads]
        pair_copy(block).start()

        @pl.when(block > 0)
        def _():
            add_pair(block - 1)

        @pl.when(block == 0)
        def _():
            key_old.start()
            value_old.start()

        return carry

    lax.fori_loop(0, ranks, score, 0)
    add_pair(ranks - 1)

    key_old.wait()
    value_old.wait()
    about = jnp.zeros((heads, HEAD_WIDTH), jnp.float32)
    position = rank * context_dev + lax.broadcasted_iota(jnp.int32, (1, context_dev), 1)
    for b in range(rows):
        old_scores = (
            lax.dot_general(
                own_queries[b], old_keys[b], (((1,), (1,)), ((), ())),
                preferred_element_type=jnp.float32,
            )
            * scale
        )
        old_scores = jnp.where(position < limits[b : b + 1, 0:1], old_scores, masked_score)
        old_peak = jnp.max(old_scores, axis=-1, keepdims=True)
        old_exact = jnp.exp(old_scores - old_peak)
        old_total = jnp.sum(old_exact, axis=-1, keepdims=True)
        old_sum = jnp.dot(
            old_exact.astype(jnp.bfloat16), old_values[b], preferred_element_type=jnp.float32
        )
        about = jnp.where(lane == b, old_peak, jnp.where(lane == rows + b, old_total, about))
        for j in range(ranks):
            h = j * local_heads // per_kv
            old[j, b] = old_sum[
                j * local_heads : (j + 1) * local_heads, h * HEAD_WIDTH : (h + 1) * HEAD_WIDTH
            ]
    for j in range(ranks):
        old[j, rows] = about[j * local_heads : (j + 1) * local_heads]

    for step in range(1, chips):
        other, peer = peer_of(step)

        def arrive(block, carry):
            remote(
                chip_sums.at[other, block],
                incoming.at[other, block],
                send_sum.at[step, block],
                got_sum.at[other, block],
                group,
                peer,
            ).wait_recv()
            return carry

        lax.fori_loop(0, ranks, arrive, 0)
    total = chip_sums[chip]
    for step in range(1, chips):
        total = total + incoming[peer_of(step)[0]]
    total = total * scale
    owner = owner_of[...]
    peaks = []
    token_peak = jnp.zeros_like(total)
    for o in range(owners):
        kept = jnp.where(owner == o, total, masked_score)
        peak = jnp.max(jnp.max(kept, axis=0), axis=-1, keepdims=True)
        peaks.append(peak)
        token_peak = jnp.where(owner == o, peak[None], token_peak)
    exact = jnp.exp(total - token_peak)
    weights[rank] = exact.astype(jnp.bfloat16)

    def weight_copy(step):
        other, peer = peer_of(step)
        return remote(
            weights.at[rank], weights.at[rank], send_weight.at[step], got_weight.at[rank], group, peer
        )

    def on_copy(step):
        other, peer = peer_of(step)
        return remote(
            weights.at[peer], weights.at[peer], send_on.at[step], got_weight.at[peer], group, partner
        )

    for step in range(1, chips):
        weight_copy(step).start()
    on_copy(0).start()
    for o in range(owners):
        amount = jnp.sum(
            jnp.sum(jnp.where(owner == o, exact, 0.0), axis=0), axis=-1, keepdims=True
        )
        stats[o] = jnp.where(lane == 0, peaks[o], jnp.where(lane == 1, amount, 0.0))
    for step in range(1, chips):
        other, peer = peer_of(step)
        remote(
            weights.at[peer], weights.at[peer], send_weight.at[step], got_weight.at[peer], group, peer
        ).wait_recv()
        on_copy(step).start()
    for step in range(chips):
        other = lax.rem(chip + step, chips) * 2 + 1 - core
        remote(
            weights.at[other], weights.at[other], send_on.at[step], got_weight.at[other], group, partner
        ).wait_recv()

    def sent(block, carry):
        pair_copy(block).wait_send()
        for step in range(1, chips):
            sum_copy(step, block).wait_send()
        return carry

    lax.fori_loop(0, ranks, sent, 0)
    for step in range(chips):
        on_copy(step).wait_send()
        if step:
            weight_copy(step).wait_send()


def fresh_weights(
    ranks, owners, scale, keys, queries, base_cos, base_sin, step_cos, step_sin, owner_of,
    cache_keys, cache_values, own_queries, limits,
):
    tokens, width = keys.shape
    tile = tokens // ranks
    rows, heads = own_queries.shape[:2]
    local_heads = heads // ranks
    chips = ranks // 2
    dma = pltpu.SemaphoreType.DMA
    vmem = pl.BlockSpec(memory_space=pltpu.VMEM)
    hbm = pl.BlockSpec(memory_space=pltpu.HBM)
    held = (chips, local_heads, tile)
    return pl.pallas_call(
        functools.partial(weight_kernel, ranks, owners, scale),
        in_specs=[hbm] + [vmem] * 6 + [hbm] * 2 + [vmem] * 2,
        out_specs=[vmem] * 3,
        out_shape=[
            jax.ShapeDtypeStruct((ranks, ranks, local_heads, tile), jnp.bfloat16),
            jax.ShapeDtypeStruct((owners, local_heads, HEAD_WIDTH), jnp.float32),
            jax.ShapeDtypeStruct((ranks, rows + 1, local_heads, HEAD_WIDTH), jnp.float32),
        ],
        scratch_shapes=[
            pltpu.VMEM((2, ranks) + held, jnp.float32),
            pltpu.VMEM((ranks,) + held, jnp.float32),
            pltpu.VMEM((chips, ranks, local_heads, tile), jnp.float32),
            pltpu.VMEM((chips, ranks, local_heads, tile), jnp.float32),
            pltpu.VMEM((2, tile, width), jnp.bfloat16),
            pltpu.VMEM((tile, width), jnp.bfloat16),
            pltpu.VMEM(cache_keys.shape, jnp.bfloat16),
            pltpu.VMEM(cache_values.shape, jnp.bfloat16),
            dma((ranks,)), dma((chips, ranks)), dma((chips,)), dma((chips,)),
            dma((ranks,)), dma((chips, ranks)), dma((ranks,)), dma((2,)), dma((2,)),
        ],
        compiler_params=pltpu.CompilerParams(
            collective_id=1, has_side_effects=True, vmem_limit_bytes=48 * 1024 * 1024
        ),
    )(
        keys, queries, base_cos, base_sin, step_cos, step_sin, owner_of,
        cache_keys, cache_values, own_queries, limits,
    )


def blend_kernel(
    groups, ranks, senders, fresh, stats, old, out, fresh_in, stats_in, old_in,
    send_fresh, send_stats, send_old, got_fresh, got_stats, got_old,
):
    group, rank = lax.axis_index("group"), lax.axis_index("tensor")
    rows = out.shape[0]
    count = groups * ranks
    own = group * ranks + rank
    greet_all(groups, ranks, group, rank)

    def peer_of(step):
        peer = lax.rem(own + step, count)
        return peer // ranks, lax.rem(peer, ranks)

    def fresh_copy(step):
        peer_group, peer_rank = peer_of(step)
        return remote(
            fresh.at[peer_group, peer_rank],
            fresh_in.at[group, rank],
            send_fresh.at[step],
            got_fresh.at[group, rank],
            peer_group,
            peer_rank,
        )

    def stats_copy(step):
        peer = lax.rem(group + step, groups)
        return remote(
            stats.at[peer], stats_in.at[group], send_stats.at[step], got_stats.at[group], peer, rank
        )

    def old_copy(step):
        peer = lax.rem(rank + step, ranks)
        return remote(
            old.at[peer], old_in.at[rank], send_old.at[step], got_old.at[rank], group, peer
        )

    for step in range(1, ranks):
        old_copy(step).start()
    for step in range(1, groups):
        stats_copy(step).start()

    def start(step, carry):
        fresh_copy(step).start()
        return carry

    lax.fori_loop(1, count, start, 0)
    old_in[rank] = old[rank]
    stats_in[group] = stats[group]
    fresh_in[group, rank] = fresh[group, rank]
    for step in range(1, ranks):
        source = lax.rem(rank + step, ranks)
        remote(
            old.at[source], old_in.at[source], send_old.at[step], got_old.at[source], group, source
        ).wait_recv()
    for step in range(1, groups):
        source = lax.rem(group + step, groups)
        remote(
            stats.at[source], stats_in.at[source], send_stats.at[step], got_stats.at[source], source, rank
        ).wait_recv()

    def finish(step, carry):
        source_group, source_rank = peer_of(step)
        remote(
            fresh.at[source_group, source_rank],
            fresh_in.at[source_group, source_rank],
            send_fresh.at[step],
            got_fresh.at[source_group, source_rank],
            source_group,
            source_rank,
        ).wait_recv()
        fresh_copy(step).wait_send()
        return carry

    lax.fori_loop(1, count, finish, 0)
    for row in range(rows):
        peaks, totals, sums = [], [], []
        for t in range(ranks):
            about = old_in[t, rows]
            peaks.append(about[:, row : row + 1])
            totals.append(about[:, rows + row : rows + row + 1])
            sums.append(old_in[t, row])
        for sender in range(row * senders, (row + 1) * senders):
            about = stats_in[sender]
            peaks.append(about[:, 0:1])
            totals.append(about[:, 1:2])
            sums.append(jnp.sum(fresh_in[sender], axis=0))
        top = functools.reduce(jnp.maximum, peaks)
        factors = [jnp.exp(peak - top) for peak in peaks]
        numerator = sum(a * b for a, b in zip(sums, factors))
        denominator = sum(a * b for a, b in zip(totals, factors))
        out[row] = (numerator / denominator).astype(out.dtype)
    for step in range(1, ranks):
        old_copy(step).wait_send()
    for step in range(1, groups):
        stats_copy(step).wait_send()


def blend(senders, fresh, stats, old):
    groups, ranks, local_heads, width = fresh.shape
    rows = old.shape[1] - 1
    dma = pltpu.SemaphoreType.DMA
    vmem = pl.BlockSpec(memory_space=pltpu.VMEM)
    return pl.pallas_call(
        functools.partial(blend_kernel, groups, ranks, senders),
        in_specs=[vmem] * 3,
        out_specs=vmem,
        out_shape=jax.ShapeDtypeStruct((rows, local_heads, width), jnp.bfloat16),
        scratch_shapes=[
            pltpu.VMEM(fresh.shape, jnp.float32),
            pltpu.VMEM(stats.shape, jnp.float32),
            pltpu.VMEM(old.shape, jnp.float32),
            dma((groups * ranks,)), dma((groups,)), dma((ranks,)),
            dma((groups, ranks)), dma((groups,)), dma((ranks,)),
        ],
        compiler_params=pltpu.CompilerParams(collective_id=2, has_side_effects=True),
    )(fresh, stats, old)


def per_device(
    prefill_states,
    key_weight,
    value_weight,
    page_slot,
    decode_states,
    query_weight,
    cache_keys,
    cache_values,
    cached_length,
):
    groups = lax.axis_size("group")
    ranks = lax.axis_size("tensor")
    group = lax.axis_index("group")
    rank = lax.axis_index("tensor")
    tokens, features = prefill_states.shape
    fresh_count = tokens // ranks
    pages = fresh_count // PAGE
    kv_heads = key_weight.shape[1] // HEAD_WIDTH
    rows = decode_states.shape[0]
    share = fresh_count // groups
    span = fresh_count // rows
    senders = span // share
    assert senders * share == span
    own_row = group // senders
    offset = (group % senders) * share
    inv_scale = 1.0 / HEAD_WIDTH**0.5

    local_queries = jnp.dot(decode_states, query_weight, preferred_element_type=jnp.float32)
    local_heads = local_queries.shape[1] // HEAD_WIDTH
    heads = local_heads * ranks
    per_kv = heads // kv_heads
    local_queries = apply_rotary(
        local_queries.reshape(rows, local_heads, HEAD_WIDTH),
        (cached_length + ranks * span)[:, None],
    ).astype(jnp.bfloat16)
    pad = jnp.zeros((1, HEAD_WIDTH), jnp.int32)
    meta = jnp.concatenate(
        [
            pad.at[0, :pages].set(page_slot.reshape(pages)),
            pad.at[0, :rows].set(cached_length),
            jnp.zeros((6, HEAD_WIDTH), jnp.int32),
        ],
        axis=0,
    )
    own_query, fresh_query, meta_ranks, meta_groups, keys = gather_queries(
        groups, ranks, senders, local_queries, meta, prefill_states, key_weight
    )
    slots = meta_ranks[:, 0, :pages]
    every_length = meta_groups[:, 1, :rows]

    per_owner = pages // groups
    fresh_length = lax.dynamic_index_in_dim(every_length, own_row, 1, keepdims=False)
    page_owner = slots // per_owner
    length_of_page = jnp.sum(
        jnp.where(
            page_owner[..., None] == jnp.arange(groups, dtype=jnp.int32), fresh_length, 0
        ),
        axis=-1,
    )
    base = (
        length_of_page
        + jnp.arange(ranks, dtype=jnp.int32)[:, None] * span
        + offset
        + (slots % per_owner) * PAGE
    )
    base_cos, base_sin = full_tables(base.reshape(-1))
    step_cos, step_sin = full_tables(jnp.arange(PAGE, dtype=jnp.int32))
    owner_of = jnp.repeat(page_owner, PAGE, axis=1).reshape(ranks, 1, fresh_count)
    own_kv = (jnp.arange(heads) // per_kv)[:, None] == jnp.arange(kv_heads)[None, :]

    def spread(query):
        query = query.reshape(-1, heads, 1, HEAD_WIDTH)
        query = jnp.where(own_kv[None, :, :, None], query, jnp.zeros_like(query))
        return query.reshape(-1, heads, kv_heads * HEAD_WIDTH)

    weights, fresh_stats, old_all = fresh_weights(
        ranks,
        groups,
        inv_scale,
        keys,
        spread(fresh_query).reshape(groups * heads, kv_heads * HEAD_WIDTH),
        base_cos,
        base_sin,
        step_cos,
        step_sin,
        owner_of,
        cache_keys,
        cache_values,
        spread(own_query.transpose(1, 0, 2, 3)),
        jnp.broadcast_to(cached_length[:, None], (rows, HEAD_WIDTH)),
    )

    weights = weights.transpose(0, 2, 1, 3).reshape(heads, tokens)
    owned = owner_of.reshape(1, 1, tokens) == jnp.arange(groups, dtype=jnp.int32)[:, None, None]
    weights = jnp.where(owned, weights[None], jnp.zeros_like(weights)[None])
    mixed = jnp.dot(
        weights.reshape(groups * heads, tokens),
        prefill_states,
        preferred_element_type=jnp.float32,
    )
    fresh_sum = jnp.einsum(
        "oknf,fkd->oknd",
        mixed.astype(jnp.bfloat16).reshape(groups, kv_heads, per_kv, features),
        value_weight.reshape(features, kv_heads, HEAD_WIDTH),
        preferred_element_type=jnp.float32,
    ).reshape(groups, ranks, local_heads, HEAD_WIDTH)

    result = blend(senders, fresh_sum, fresh_stats, old_all)
    return result.reshape(rows, local_heads * HEAD_WIDTH)


def solution(mesh):
    placed = (
        P("group", "tensor"),
        P("tensor", None),
        P("tensor", None),
        P("group", "tensor", None),
        P("group", None),
        P(None, "tensor"),
        P("group", "tensor", None),
        P("group", "tensor", None),
        P("group"),
    )
    return jax.shard_map(
        per_device, mesh=mesh, in_specs=placed, out_specs=P("group", "tensor"), check_vma=False
    )
```

```python
import functools

import jax
import jax.numpy as jnp
from jax import lax
from jax.experimental import pallas as pl
from jax.experimental.pallas import tpu as pltpu
from jax.sharding import PartitionSpec as P

HEAD_WIDTH = 128
PAGE = 8


rope_theta = 500000.0
masked_score = -1e30


def angles_of(positions):
    half_width = HEAD_WIDTH // 2
    index_float = jnp.arange(half_width, dtype=jnp.float32)
    frequency = rope_theta ** (-2.0 * index_float / HEAD_WIDTH)
    return positions[..., None].astype(jnp.float32) * frequency


def full_tables(positions):
    angles = angles_of(positions)
    cosine_part = jnp.cos(angles)
    sine_part = jnp.sin(angles)
    return (
        jnp.concatenate([cosine_part, cosine_part], axis=-1),
        jnp.concatenate([sine_part, sine_part], axis=-1),
    )


def apply_rotary(vectors, positions):
    half_width = vectors.shape[-1] // 2
    angles = angles_of(positions)
    cosine_part = jnp.cos(angles)
    sine_part = jnp.sin(angles)
    first_half = vectors[..., :half_width]
    second_half = vectors[..., half_width:]
    return jnp.concatenate(
        [
            first_half * cosine_part - second_half * sine_part,
            second_half * cosine_part + first_half * sine_part,
        ],
        axis=-1,
    )


def remote(src, dst, send_sem, recv_sem, group, rank):
    return pltpu.make_async_remote_copy(
        src_ref=src,
        dst_ref=dst,
        send_sem=send_sem,
        recv_sem=recv_sem,
        device_id={"group": group, "tensor": rank},
        device_id_type=pl.DeviceIdType.MESH,
    )


def greet_all(groups, ranks, group, rank):
    barrier = pltpu.get_barrier_semaphore()
    count = groups * ranks
    own = group * ranks + rank

    def greet(step, carry):
        peer = lax.rem(own + step, count)
        pl.semaphore_signal(
            barrier,
            inc=1,
            device_id={"group": peer // ranks, "tensor": lax.rem(peer, ranks)},
            device_id_type=pl.DeviceIdType.MESH,
        )
        return carry

    lax.fori_loop(1, count, greet, 0)
    pl.semaphore_wait(barrier, count - 1)


def gather_kernel(
    groups, ranks, senders, query, meta, states, weight,
    own_query, fresh_query, meta_ranks, meta_groups, keys,
    send_query, send_fresh, send_ranks, send_groups, got_query, got_fresh, got_ranks, got_groups,
    state_tiles, key_tiles, state_sems, key_sems,
):
    group, rank = lax.axis_index("group"), lax.axis_index("tensor")
    tile = state_tiles.shape[1]
    tiles = states.shape[0] // tile

    def state_copy(step, slot):
        start = pl.multiple_of(step * tile, tile)
        return pltpu.make_async_copy(
            states.at[pl.ds(start, tile), :], state_tiles.at[slot], state_sems.at[slot]
        )

    def key_copy(step, slot):
        start = pl.multiple_of(step * tile, tile)
        return pltpu.make_async_copy(
            key_tiles.at[slot], keys.at[pl.ds(start, tile), :], key_sems.at[slot]
        )

    state_copy(0, 0).start()
    greet_all(groups, ranks, group, rank)

    def to_rank(step):
        peer = lax.rem(rank + step, ranks)
        return (
            remote(
                meta, meta_ranks.at[rank], send_ranks.at[step], got_ranks.at[rank], group, peer
            ),
            remote(
                query, own_query.at[rank], send_query.at[step], got_query.at[rank], group, peer
            ),
        )

    def to_group(step):
        peer = lax.rem(group + step, groups)
        return remote(
            meta, meta_groups.at[group], send_groups.at[step], got_groups.at[group], peer, rank
        )

    def to_fresh(step):
        peer_group = lax.rem(group + 1 + step // ranks, groups)
        peer_rank = lax.rem(rank + step, ranks)
        return remote(
            query.at[peer_group // senders],
            fresh_query.at[group, rank],
            send_fresh.at[step],
            got_fresh.at[group, rank],
            peer_group,
            peer_rank,
        )

    for step in range(1, ranks):
        for copy in to_rank(step):
            copy.start()
    for step in range(1, groups):
        to_group(step).start()

    def start(step, carry):
        to_fresh(step).start()
        return carry

    lax.fori_loop(0, (groups - 1) * ranks, start, 0)
    own_query[rank] = query[...]
    meta_ranks[rank] = meta[...]
    meta_groups[group] = meta[...]

    def project(step, carry):
        slot = lax.rem(step, 2)

        @pl.when(step + 1 < tiles)
        def _():
            state_copy(step + 1, 1 - slot).start()

        state_copy(step, slot).wait()

        @pl.when(step >= 2)
        def _():
            key_copy(step - 2, slot).wait()

        key_tiles[slot] = jnp.dot(
            state_tiles[slot], weight[...], preferred_element_type=jnp.float32
        ).astype(jnp.bfloat16)
        key_copy(step, slot).start()
        return carry

    lax.fori_loop(0, tiles, project, 0)
    key_copy(tiles - 2, (tiles - 2) % 2).wait()
    key_copy(tiles - 1, (tiles - 1) % 2).wait()
    for step in range(1, ranks):
        source = lax.rem(rank + step, ranks)
        remote(
            query, own_query.at[source], send_query.at[step], got_query.at[source], group, source
        ).wait_recv()
        remote(
            meta, meta_ranks.at[source], send_ranks.at[step], got_ranks.at[source], group, source
        ).wait_recv()
    for step in range(1, groups):
        source = lax.rem(group + step, groups)
        remote(
            meta, meta_groups.at[source], send_groups.at[step], got_groups.at[source], source, rank
        ).wait_recv()
    for t in range(ranks):
        fresh_query[group, t] = own_query[t, group // senders]

    def finish(step, carry):
        source_group = lax.rem(group + 1 + step // ranks, groups)
        source_rank = lax.rem(rank + step, ranks)
        remote(
            query.at[0],
            fresh_query.at[source_group, source_rank],
            send_fresh.at[step],
            got_fresh.at[source_group, source_rank],
            source_group,
            source_rank,
        ).wait_recv()
        to_fresh(step).wait_send()
        return carry

    lax.fori_loop(0, (groups - 1) * ranks, finish, 0)
    for step in range(1, ranks):
        for copy in to_rank(step):
            copy.wait_send()
    for step in range(1, groups):
        to_group(step).wait_send()


def gather_queries(groups, ranks, senders, query, meta, states, weight):
    rows, local_heads, width = query.shape
    dma = pltpu.SemaphoreType.DMA
    others = (groups - 1) * ranks
    tokens, features = states.shape
    tile = tokens // ranks
    hbm = pl.BlockSpec(memory_space=pltpu.HBM)
    vmem = pl.BlockSpec(memory_space=pltpu.VMEM)
    return pl.pallas_call(
        functools.partial(gather_kernel, groups, ranks, senders),
        in_specs=[vmem, vmem, hbm, vmem],
        out_specs=[vmem] * 4 + [pl.BlockSpec(memory_space=pl.ANY)],
        out_shape=[
            jax.ShapeDtypeStruct((ranks, rows, local_heads, width), query.dtype),
            jax.ShapeDtypeStruct((groups, ranks, local_heads, width), query.dtype),
            jax.ShapeDtypeStruct((ranks,) + meta.shape, meta.dtype),
            jax.ShapeDtypeStruct((groups,) + meta.shape, meta.dtype),
            jax.ShapeDtypeStruct((tokens, weight.shape[1]), jnp.bfloat16),
        ],
        scratch_shapes=[
            dma((ranks,)), dma((others,)), dma((ranks,)), dma((groups,)),
            dma((ranks,)), dma((groups, ranks)), dma((ranks,)), dma((groups,)),
            pltpu.VMEM((2, tile, features), jnp.bfloat16),
            pltpu.VMEM((2, tile, weight.shape[1]), jnp.bfloat16),
            dma((2,)), dma((2,)),
        ],
        compiler_params=pltpu.CompilerParams(
            collective_id=0, has_side_effects=True, vmem_limit_bytes=60 * 1024 * 1024
        ),
    )(query, meta, states, weight)


def weight_kernel(
    ranks, owners, scale, keys, queries, base_cos, base_sin, step_cos, step_sin, owner_of,
    cache_keys, cache_values, own_queries, limits,
    weights, stats, old,
    partial_scores, paired, chip_sums, incoming, key_tiles, turned, old_keys, old_values, old_own,
    send_pair, send_sum, send_weight, send_on, got_pair, got_sum, got_weight, key_sems, old_sems,
    send_old, got_old,
):
    group, rank = lax.axis_index("group"), lax.axis_index("tensor")
    chips = ranks // 2
    core, chip = lax.rem(rank, 2), rank // 2
    partner = chip * 2 + 1 - core
    tile = turned.shape[0]
    local_heads = weights.shape[2]
    heads = local_heads * ranks
    kv_heads = turned.shape[1] // HEAD_WIDTH
    per_kv = heads // kv_heads
    rows, context_dev = cache_keys.shape[:2]
    pages = tile // PAGE

    def key_copy(step, slot):
        start = pl.multiple_of(step * tile, tile)
        return pltpu.make_async_copy(
            keys.at[pl.ds(start, tile), :], key_tiles.at[slot], key_sems.at[slot]
        )

    key_copy(0, 0).start()
    barrier = pltpu.get_barrier_semaphore()

    def peer_of(step):
        other = lax.rem(chip + step, chips)
        return other, other * 2 + core

    for peer in [lax.rem(rank + step, ranks) for step in range(1, ranks)]:
        pl.semaphore_signal(
            barrier,
            inc=1,
            device_id={"group": group, "tensor": peer},
            device_id_type=pl.DeviceIdType.MESH,
        )
    key_old = pltpu.make_async_copy(cache_keys, old_keys, old_sems.at[0])
    value_old = pltpu.make_async_copy(cache_values, old_values, old_sems.at[1])
    pl.semaphore_wait(barrier, ranks - 1)

    def pair_copy(block):
        return remote(
            partial_scores.at[1 - core, block],
            paired.at[block],
            send_pair.at[block],
            got_pair.at[block],
            group,
            partner,
        )

    def sum_copy(step, block):
        other, peer = peer_of(step)
        return remote(
            chip_sums.at[other, block],
            incoming.at[chip, block],
            send_sum.at[step, block],
            got_sum.at[chip, block],
            group,
            peer,
        )

    def add_pair(block):
        pair_copy(block).wait_recv()
        for step in range(1, chips):
            other, peer = peer_of(step)
            chip_sums[other, block] = partial_scores[core, block, other] + paired[block, other]
            sum_copy(step, block).start()
        chip_sums[chip, block] = partial_scores[core, block, chip] + paired[block, chip]

    lane = lax.broadcasted_iota(jnp.int32, (1, HEAD_WIDTH), 1)
    sign = jnp.where(lane < HEAD_WIDTH // 2, -1.0, 1.0).astype(jnp.float32)

    def score(block, carry):
        slot = lax.rem(block, 2)

        @pl.when(block + 1 < ranks)
        def _():
            key_copy(block + 1, 1 - slot).start()

        key_copy(block, slot).wait()
        span = pl.ds(pl.multiple_of(block * pages, pages), pages)
        big_cos = base_cos[span, :].reshape(pages, 1, HEAD_WIDTH)
        big_sin = base_sin[span, :].reshape(pages, 1, HEAD_WIDTH)
        small_cos = step_cos[...].reshape(1, PAGE, HEAD_WIDTH)
        small_sin = step_sin[...].reshape(1, PAGE, HEAD_WIDTH)
        cosine = (big_cos * small_cos - big_sin * small_sin).reshape(tile, HEAD_WIDTH)
        sine = (big_sin * small_cos + big_cos * small_sin).reshape(tile, HEAD_WIDTH) * sign
        for h in range(kv_heads):
            columns = slice(h * HEAD_WIDTH, (h + 1) * HEAD_WIDTH)
            head = key_tiles[slot, :, columns].astype(jnp.float32)
            turned[:, columns] = (
                head * cosine + pltpu.roll(head, HEAD_WIDTH // 2, 1) * sine
            ).astype(jnp.bfloat16)
        found = lax.dot_general(
            queries[...], turned[...], (((1,), (1,)), ((), ())), preferred_element_type=jnp.float32
        )
        owner = owner_of[block]
        kept = jnp.zeros((heads, tile), jnp.float32)
        for o in range(owners):
            kept = jnp.where(owner == o, found[o * heads : (o + 1) * heads], kept)
        for j in range(ranks):
            partial_scores[j % 2, block, j // 2] = kept[j * local_heads : (j + 1) * local_heads]
        pair_copy(block).start()

        @pl.when(block > 0)
        def _():
            add_pair(block - 1)

        @pl.when(block == 0)
        def _():
            key_old.start()
            value_old.start()

        return carry

    lax.fori_loop(0, ranks, score, 0)
    add_pair(ranks - 1)

    key_old.wait()
    value_old.wait()
    about = jnp.zeros((heads, HEAD_WIDTH), jnp.float32)
    position = rank * context_dev + lax.broadcasted_iota(jnp.int32, (1, context_dev), 1)
    for b in range(rows):
        old_scores = (
            lax.dot_general(
                own_queries[b], old_keys[b], (((1,), (1,)), ((), ())),
                preferred_element_type=jnp.float32,
            )
            * scale
        )
        old_scores = jnp.where(position < limits[b : b + 1, 0:1], old_scores, masked_score)
        old_peak = jnp.max(old_scores, axis=-1, keepdims=True)
        old_exact = jnp.exp(old_scores - old_peak)
        old_total = jnp.sum(old_exact, axis=-1, keepdims=True)
        old_sum = jnp.dot(
            old_exact.astype(jnp.bfloat16), old_values[b], preferred_element_type=jnp.float32
        )
        about = jnp.where(lane == b, old_peak, jnp.where(lane == rows + b, old_total, about))
        for j in range(ranks):
            h = j * local_heads // per_kv
            old_own[j, b] = old_sum[
                j * local_heads : (j + 1) * local_heads, h * HEAD_WIDTH : (h + 1) * HEAD_WIDTH
            ]
    for j in range(ranks):
        old_own[j, rows] = about[j * local_heads : (j + 1) * local_heads]

    def old_copy(step):
        peer = lax.rem(rank + step, ranks)
        return remote(
            old_own.at[peer], old.at[rank], send_old.at[step], got_old.at[rank], group, peer
        )

    for step in range(1, ranks):
        old_copy(step).start()
    old[rank] = old_own[rank]

    for step in range(1, chips):
        other, peer = peer_of(step)

        def arrive(block, carry):
            remote(
                chip_sums.at[other, block],
                incoming.at[other, block],
                send_sum.at[step, block],
                got_sum.at[other, block],
                group,
                peer,
            ).wait_recv()
            return carry

        lax.fori_loop(0, ranks, arrive, 0)
    total = chip_sums[chip]
    for step in range(1, chips):
        total = total + incoming[peer_of(step)[0]]
    total = total * scale
    owner = owner_of[...]
    peaks = []
    token_peak = jnp.zeros_like(total)
    for o in range(owners):
        kept = jnp.where(owner == o, total, masked_score)
        peak = jnp.max(jnp.max(kept, axis=0), axis=-1, keepdims=True)
        peaks.append(peak)
        token_peak = jnp.where(owner == o, peak[None], token_peak)
    exact = jnp.exp(total - token_peak)
    weights[rank] = exact.astype(jnp.bfloat16)

    def weight_copy(step):
        other, peer = peer_of(step)
        return remote(
            weights.at[rank], weights.at[rank], send_weight.at[step], got_weight.at[rank], group, peer
        )

    def on_copy(step):
        other, peer = peer_of(step)
        return remote(
            weights.at[peer], weights.at[peer], send_on.at[step], got_weight.at[peer], group, partner
        )

    for step in range(1, chips):
        weight_copy(step).start()
    on_copy(0).start()
    for o in range(owners):
        amount = jnp.sum(
            jnp.sum(jnp.where(owner == o, exact, 0.0), axis=0), axis=-1, keepdims=True
        )
        stats[o] = jnp.where(lane == 0, peaks[o], jnp.where(lane == 1, amount, 0.0))
    for step in range(1, chips):
        other, peer = peer_of(step)
        remote(
            weights.at[peer], weights.at[peer], send_weight.at[step], got_weight.at[peer], group, peer
        ).wait_recv()
        on_copy(step).start()
    for step in range(chips):
        other = lax.rem(chip + step, chips) * 2 + 1 - core
        remote(
            weights.at[other], weights.at[other], send_on.at[step], got_weight.at[other], group, partner
        ).wait_recv()

    def sent(block, carry):
        pair_copy(block).wait_send()
        for step in range(1, chips):
            sum_copy(step, block).wait_send()
        return carry

    lax.fori_loop(0, ranks, sent, 0)
    for step in range(1, ranks):
        source = lax.rem(rank + step, ranks)
        remote(
            old_own.at[source], old.at[source], send_old.at[step], got_old.at[source], group, source
        ).wait_recv()
        old_copy(step).wait_send()
    for step in range(chips):
        on_copy(step).wait_send()
        if step:
            weight_copy(step).wait_send()


def fresh_weights(
    ranks, owners, scale, keys, queries, base_cos, base_sin, step_cos, step_sin, owner_of,
    cache_keys, cache_values, own_queries, limits,
):
    tokens, width = keys.shape
    tile = tokens // ranks
    rows, heads = own_queries.shape[:2]
    local_heads = heads // ranks
    chips = ranks // 2
    dma = pltpu.SemaphoreType.DMA
    vmem = pl.BlockSpec(memory_space=pltpu.VMEM)
    hbm = pl.BlockSpec(memory_space=pltpu.HBM)
    held = (chips, local_heads, tile)
    return pl.pallas_call(
        functools.partial(weight_kernel, ranks, owners, scale),
        in_specs=[pl.BlockSpec(memory_space=pl.ANY)] + [vmem] * 6 + [hbm] * 2 + [vmem] * 2,
        out_specs=[vmem] * 3,
        out_shape=[
            jax.ShapeDtypeStruct((ranks, ranks, local_heads, tile), jnp.bfloat16),
            jax.ShapeDtypeStruct((owners, local_heads, HEAD_WIDTH), jnp.float32),
            jax.ShapeDtypeStruct((ranks, rows + 1, local_heads, HEAD_WIDTH), jnp.float32),
        ],
        scratch_shapes=[
            pltpu.VMEM((2, ranks) + held, jnp.float32),
            pltpu.VMEM((ranks,) + held, jnp.float32),
            pltpu.VMEM((chips, ranks, local_heads, tile), jnp.float32),
            pltpu.VMEM((chips, ranks, local_heads, tile), jnp.float32),
            pltpu.VMEM((2, tile, width), jnp.bfloat16),
            pltpu.VMEM((tile, width), jnp.bfloat16),
            pltpu.VMEM(cache_keys.shape, jnp.bfloat16),
            pltpu.VMEM(cache_values.shape, jnp.bfloat16),
            pltpu.VMEM((ranks, rows + 1, local_heads, HEAD_WIDTH), jnp.float32),
            dma((ranks,)), dma((chips, ranks)), dma((chips,)), dma((chips,)),
            dma((ranks,)), dma((chips, ranks)), dma((ranks,)), dma((2,)), dma((2,)),
            dma((ranks,)), dma((ranks,)),
        ],
        compiler_params=pltpu.CompilerParams(
            collective_id=1, has_side_effects=True, vmem_limit_bytes=28 * 1024 * 1024
        ),
    )(
        keys, queries, base_cos, base_sin, step_cos, step_sin, owner_of,
        cache_keys, cache_values, own_queries, limits,
    )


def blend_kernel(
    groups, ranks, senders, fresh, stats, old_in, out, fresh_in, stats_in,
    send_fresh, send_stats, got_fresh, got_stats,
):
    group, rank = lax.axis_index("group"), lax.axis_index("tensor")
    rows = out.shape[0]
    count = groups * ranks
    own = group * ranks + rank
    greet_all(groups, ranks, group, rank)

    def peer_of(step):
        peer = lax.rem(own + step, count)
        return peer // ranks, lax.rem(peer, ranks)

    def fresh_copy(step):
        peer_group, peer_rank = peer_of(step)
        return remote(
            fresh.at[peer_group, peer_rank],
            fresh_in.at[group, rank],
            send_fresh.at[step],
            got_fresh.at[group, rank],
            peer_group,
            peer_rank,
        )

    def stats_copy(step):
        peer = lax.rem(group + step, groups)
        return remote(
            stats.at[peer], stats_in.at[group], send_stats.at[step], got_stats.at[group], peer, rank
        )

    for step in range(1, groups):
        stats_copy(step).start()

    def start(step, carry):
        fresh_copy(step).start()
        return carry

    lax.fori_loop(1, count, start, 0)
    stats_in[group] = stats[group]
    fresh_in[group, rank] = fresh[group, rank]
    for step in range(1, groups):
        source = lax.rem(group + step, groups)
        remote(
            stats.at[source], stats_in.at[source], send_stats.at[step], got_stats.at[source], source, rank
        ).wait_recv()

    def finish(step, carry):
        source_group, source_rank = peer_of(step)
        remote(
            fresh.at[source_group, source_rank],
            fresh_in.at[source_group, source_rank],
            send_fresh.at[step],
            got_fresh.at[source_group, source_rank],
            source_group,
            source_rank,
        ).wait_recv()
        fresh_copy(step).wait_send()
        return carry

    lax.fori_loop(1, count, finish, 0)
    for row in range(rows):
        peaks, totals, sums = [], [], []
        for t in range(ranks):
            about = old_in[t, rows]
            peaks.append(about[:, row : row + 1])
            totals.append(about[:, rows + row : rows + row + 1])
            sums.append(old_in[t, row])
        for sender in range(row * senders, (row + 1) * senders):
            about = stats_in[sender]
            peaks.append(about[:, 0:1])
            totals.append(about[:, 1:2])
            sums.append(jnp.sum(fresh_in[sender], axis=0))
        top = functools.reduce(jnp.maximum, peaks)
        factors = [jnp.exp(peak - top) for peak in peaks]
        numerator = sum(a * b for a, b in zip(sums, factors))
        denominator = sum(a * b for a, b in zip(totals, factors))
        out[row] = (numerator / denominator).astype(out.dtype)
    for step in range(1, groups):
        stats_copy(step).wait_send()


def blend(senders, fresh, stats, old):
    groups, ranks, local_heads, width = fresh.shape
    rows = old.shape[1] - 1
    dma = pltpu.SemaphoreType.DMA
    vmem = pl.BlockSpec(memory_space=pltpu.VMEM)
    return pl.pallas_call(
        functools.partial(blend_kernel, groups, ranks, senders),
        in_specs=[vmem] * 3,
        out_specs=vmem,
        out_shape=jax.ShapeDtypeStruct((rows, local_heads, width), jnp.bfloat16),
        scratch_shapes=[
            pltpu.VMEM(fresh.shape, jnp.float32),
            pltpu.VMEM(stats.shape, jnp.float32),
            dma((groups * ranks,)), dma((groups,)), dma((groups, ranks)), dma((groups,)),
        ],
        compiler_params=pltpu.CompilerParams(collective_id=2, has_side_effects=True),
    )(fresh, stats, old)


def per_device(
    prefill_states,
    key_weight,
    value_weight,
    page_slot,
    decode_states,
    query_weight,
    cache_keys,
    cache_values,
    cached_length,
):
    groups = lax.axis_size("group")
    ranks = lax.axis_size("tensor")
    group = lax.axis_index("group")
    rank = lax.axis_index("tensor")
    tokens, features = prefill_states.shape
    fresh_count = tokens // ranks
    pages = fresh_count // PAGE
    kv_heads = key_weight.shape[1] // HEAD_WIDTH
    rows = decode_states.shape[0]
    share = fresh_count // groups
    span = fresh_count // rows
    senders = span // share
    assert senders * share == span
    own_row = group // senders
    offset = (group % senders) * share
    inv_scale = 1.0 / HEAD_WIDTH**0.5

    local_queries = jnp.dot(decode_states, query_weight, preferred_element_type=jnp.float32)
    local_heads = local_queries.shape[1] // HEAD_WIDTH
    heads = local_heads * ranks
    per_kv = heads // kv_heads
    local_queries = apply_rotary(
        local_queries.reshape(rows, local_heads, HEAD_WIDTH),
        (cached_length + ranks * span)[:, None],
    ).astype(jnp.bfloat16)
    pad = jnp.zeros((1, HEAD_WIDTH), jnp.int32)
    meta = jnp.concatenate(
        [
            pad.at[0, :pages].set(page_slot.reshape(pages)),
            pad.at[0, :rows].set(cached_length),
            jnp.zeros((6, HEAD_WIDTH), jnp.int32),
        ],
        axis=0,
    )
    own_query, fresh_query, meta_ranks, meta_groups, keys = gather_queries(
        groups, ranks, senders, local_queries, meta, prefill_states, key_weight
    )
    slots = meta_ranks[:, 0, :pages]
    every_length = meta_groups[:, 1, :rows]

    per_owner = pages // groups
    fresh_length = lax.dynamic_index_in_dim(every_length, own_row, 1, keepdims=False)
    page_owner = slots // per_owner
    length_of_page = jnp.sum(
        jnp.where(
            page_owner[..., None] == jnp.arange(groups, dtype=jnp.int32), fresh_length, 0
        ),
        axis=-1,
    )
    base = (
        length_of_page
        + jnp.arange(ranks, dtype=jnp.int32)[:, None] * span
        + offset
        + (slots % per_owner) * PAGE
    )
    base_cos, base_sin = full_tables(base.reshape(-1))
    step_cos, step_sin = full_tables(jnp.arange(PAGE, dtype=jnp.int32))
    owner_of = jnp.repeat(page_owner, PAGE, axis=1).reshape(ranks, 1, fresh_count)
    own_kv = (jnp.arange(heads) // per_kv)[:, None] == jnp.arange(kv_heads)[None, :]

    def spread(query):
        query = query.reshape(-1, heads, 1, HEAD_WIDTH)
        query = jnp.where(own_kv[None, :, :, None], query, jnp.zeros_like(query))
        return query.reshape(-1, heads, kv_heads * HEAD_WIDTH)

    weights, fresh_stats, old_all = fresh_weights(
        ranks,
        groups,
        inv_scale,
        keys,
        spread(fresh_query).reshape(groups * heads, kv_heads * HEAD_WIDTH),
        base_cos,
        base_sin,
        step_cos,
        step_sin,
        owner_of,
        cache_keys,
        cache_values,
        spread(own_query.transpose(1, 0, 2, 3)),
        jnp.broadcast_to(cached_length[:, None], (rows, HEAD_WIDTH)),
    )

    weights = weights.transpose(0, 2, 1, 3).reshape(heads, tokens)
    owned = owner_of.reshape(1, 1, tokens) == jnp.arange(groups, dtype=jnp.int32)[:, None, None]
    weights = jnp.where(owned, weights[None], jnp.zeros_like(weights)[None])
    mixed = jnp.dot(
        weights.reshape(groups * heads, tokens),
        prefill_states,
        preferred_element_type=jnp.float32,
    )
    fresh_sum = jnp.einsum(
        "oknf,fkd->oknd",
        mixed.astype(jnp.bfloat16).reshape(groups, kv_heads, per_kv, features),
        value_weight.reshape(features, kv_heads, HEAD_WIDTH),
        preferred_element_type=jnp.float32,
    ).reshape(groups, ranks, local_heads, HEAD_WIDTH)

    result = blend(senders, fresh_sum, fresh_stats, old_all)
    return result.reshape(rows, local_heads * HEAD_WIDTH)


def solution(mesh):
    placed = (
        P("group", "tensor"),
        P("tensor", None),
        P("tensor", None),
        P("group", "tensor", None),
        P("group", None),
        P(None, "tensor"),
        P("group", "tensor", None),
        P("group", "tensor", None),
        P("group"),
    )
    return jax.shard_map(
        per_device, mesh=mesh, in_specs=placed, out_specs=P("group", "tensor"), check_vma=False
    )
```

```python
import functools

import jax
import jax.numpy as jnp
from jax import lax
from jax.experimental import pallas as pl
from jax.experimental.pallas import tpu as pltpu
from jax.sharding import PartitionSpec as P

HEAD_WIDTH = 128
PAGE = 8


rope_theta = 500000.0
masked_score = -1e30


def angles_of(positions):
    half_width = HEAD_WIDTH // 2
    index_float = jnp.arange(half_width, dtype=jnp.float32)
    frequency = rope_theta ** (-2.0 * index_float / HEAD_WIDTH)
    return positions[..., None].astype(jnp.float32) * frequency


def full_tables(positions):
    angles = angles_of(positions)
    cosine_part = jnp.cos(angles)
    sine_part = jnp.sin(angles)
    return (
        jnp.concatenate([cosine_part, cosine_part], axis=-1),
        jnp.concatenate([sine_part, sine_part], axis=-1),
    )


def apply_rotary(vectors, positions):
    half_width = vectors.shape[-1] // 2
    angles = angles_of(positions)
    cosine_part = jnp.cos(angles)
    sine_part = jnp.sin(angles)
    first_half = vectors[..., :half_width]
    second_half = vectors[..., half_width:]
    return jnp.concatenate(
        [
            first_half * cosine_part - second_half * sine_part,
            second_half * cosine_part + first_half * sine_part,
        ],
        axis=-1,
    )


def remote(src, dst, send_sem, recv_sem, group, rank):
    return pltpu.make_async_remote_copy(
        src_ref=src,
        dst_ref=dst,
        send_sem=send_sem,
        recv_sem=recv_sem,
        device_id={"group": group, "tensor": rank},
        device_id_type=pl.DeviceIdType.MESH,
    )


def greet_all(groups, ranks, group, rank):
    barrier = pltpu.get_barrier_semaphore()
    count = groups * ranks
    own = group * ranks + rank

    def greet(step, carry):
        peer = lax.rem(own + step, count)
        pl.semaphore_signal(
            barrier,
            inc=1,
            device_id={"group": peer // ranks, "tensor": lax.rem(peer, ranks)},
            device_id_type=pl.DeviceIdType.MESH,
        )
        return carry

    lax.fori_loop(1, count, greet, 0)
    pl.semaphore_wait(barrier, count - 1)


def gather_kernel(
    groups, ranks, senders, query, meta, states, weight,
    own_query, fresh_query, meta_ranks, meta_groups, keys,
    send_query, send_fresh, send_ranks, send_groups, got_query, got_fresh, got_ranks, got_groups,
    state_tiles, key_tiles, state_sems, key_sems,
):
    group, rank = lax.axis_index("group"), lax.axis_index("tensor")
    tile = state_tiles.shape[1]
    tiles = states.shape[0] // tile

    def state_copy(step, slot):
        start = pl.multiple_of(step * tile, tile)
        return pltpu.make_async_copy(
            states.at[pl.ds(start, tile), :], state_tiles.at[slot], state_sems.at[slot]
        )

    def key_copy(step, slot):
        start = pl.multiple_of(step * tile, tile)
        return pltpu.make_async_copy(
            key_tiles.at[slot], keys.at[pl.ds(start, tile), :], key_sems.at[slot]
        )

    state_copy(0, 0).start()
    greet_all(groups, ranks, group, rank)

    def to_rank(step):
        peer = lax.rem(rank + step, ranks)
        return (
            remote(
                meta, meta_ranks.at[rank], send_ranks.at[step], got_ranks.at[rank], group, peer
            ),
            remote(
                query, own_query.at[rank], send_query.at[step], got_query.at[rank], group, peer
            ),
        )

    def to_group(step):
        peer = lax.rem(group + step, groups)
        return remote(
            meta, meta_groups.at[group], send_groups.at[step], got_groups.at[group], peer, rank
        )

    def to_fresh(step):
        peer_group = lax.rem(group + 1 + step // ranks, groups)
        peer_rank = lax.rem(rank + step, ranks)
        return remote(
            query.at[peer_group // senders],
            fresh_query.at[group, rank],
            send_fresh.at[step],
            got_fresh.at[group, rank],
            peer_group,
            peer_rank,
        )

    for step in range(1, ranks):
        for copy in to_rank(step):
            copy.start()
    for step in range(1, groups):
        to_group(step).start()

    def start(step, carry):
        to_fresh(step).start()
        return carry

    lax.fori_loop(0, (groups - 1) * ranks, start, 0)
    own_query[rank] = query[...]
    meta_ranks[rank] = meta[...]
    meta_groups[group] = meta[...]

    def project(step, carry):
        slot = lax.rem(step, 2)

        @pl.when(step + 1 < tiles)
        def _():
            state_copy(step + 1, 1 - slot).start()

        state_copy(step, slot).wait()

        @pl.when(step >= 2)
        def _():
            key_copy(step - 2, slot).wait()

        key_tiles[slot] = jnp.dot(
            state_tiles[slot], weight[...], preferred_element_type=jnp.float32
        ).astype(jnp.bfloat16)
        key_copy(step, slot).start()
        return carry

    lax.fori_loop(0, tiles, project, 0)
    key_copy(tiles - 2, (tiles - 2) % 2).wait()
    key_copy(tiles - 1, (tiles - 1) % 2).wait()
    for step in range(1, ranks):
        source = lax.rem(rank + step, ranks)
        remote(
            query, own_query.at[source], send_query.at[step], got_query.at[source], group, source
        ).wait_recv()
        remote(
            meta, meta_ranks.at[source], send_ranks.at[step], got_ranks.at[source], group, source
        ).wait_recv()
    for step in range(1, groups):
        source = lax.rem(group + step, groups)
        remote(
            meta, meta_groups.at[source], send_groups.at[step], got_groups.at[source], source, rank
        ).wait_recv()
    for t in range(ranks):
        fresh_query[group, t] = own_query[t, group // senders]

    def finish(step, carry):
        source_group = lax.rem(group + 1 + step // ranks, groups)
        source_rank = lax.rem(rank + step, ranks)
        remote(
            query.at[0],
            fresh_query.at[source_group, source_rank],
            send_fresh.at[step],
            got_fresh.at[source_group, source_rank],
            source_group,
            source_rank,
        ).wait_recv()
        to_fresh(step).wait_send()
        return carry

    lax.fori_loop(0, (groups - 1) * ranks, finish, 0)
    for step in range(1, ranks):
        for copy in to_rank(step):
            copy.wait_send()
    for step in range(1, groups):
        to_group(step).wait_send()


def gather_queries(groups, ranks, senders, query, meta, states, weight):
    rows, local_heads, width = query.shape
    dma = pltpu.SemaphoreType.DMA
    others = (groups - 1) * ranks
    tokens, features = states.shape
    tile = tokens // ranks
    hbm = pl.BlockSpec(memory_space=pltpu.HBM)
    vmem = pl.BlockSpec(memory_space=pltpu.VMEM)
    return pl.pallas_call(
        functools.partial(gather_kernel, groups, ranks, senders),
        in_specs=[vmem, vmem, hbm, vmem],
        out_specs=[vmem] * 4 + [pl.BlockSpec(memory_space=pl.ANY)],
        out_shape=[
            jax.ShapeDtypeStruct((ranks, rows, local_heads, width), query.dtype),
            jax.ShapeDtypeStruct((groups, ranks, local_heads, width), query.dtype),
            jax.ShapeDtypeStruct((ranks,) + meta.shape, meta.dtype),
            jax.ShapeDtypeStruct((groups,) + meta.shape, meta.dtype),
            jax.ShapeDtypeStruct((tokens, weight.shape[1]), jnp.bfloat16),
        ],
        scratch_shapes=[
            dma((ranks,)), dma((others,)), dma((ranks,)), dma((groups,)),
            dma((ranks,)), dma((groups, ranks)), dma((ranks,)), dma((groups,)),
            pltpu.VMEM((2, tile, features), jnp.bfloat16),
            pltpu.VMEM((2, tile, weight.shape[1]), jnp.bfloat16),
            dma((2,)), dma((2,)),
        ],
        compiler_params=pltpu.CompilerParams(
            collective_id=0, has_side_effects=True, vmem_limit_bytes=60 * 1024 * 1024
        ),
    )(query, meta, states, weight)


def weight_kernel(
    ranks, owners, scale, keys, queries, base_cos, base_sin, step_cos, step_sin, owner_of,
    cache_keys, cache_values, own_queries, limits,
    weights, stats, old,
    partial_scores, paired, chip_sums, incoming, key_tiles, turned, old_keys, old_values, old_own,
    send_pair, send_sum, send_weight, send_on, got_pair, got_sum, got_weight, key_sems, old_sems,
    send_old, got_old,
):
    group, rank = lax.axis_index("group"), lax.axis_index("tensor")
    chips = ranks // 2
    core, chip = lax.rem(rank, 2), rank // 2
    partner = chip * 2 + 1 - core
    tile = turned.shape[0]
    local_heads = weights.shape[2]
    heads = local_heads * ranks
    kv_heads = turned.shape[1] // HEAD_WIDTH
    per_kv = heads // kv_heads
    rows, context_dev = cache_keys.shape[:2]
    pages = tile // PAGE

    def key_copy(step, slot):
        start = pl.multiple_of(step * tile, tile)
        return pltpu.make_async_copy(
            keys.at[pl.ds(start, tile), :], key_tiles.at[slot], key_sems.at[slot]
        )

    key_copy(0, 0).start()
    barrier = pltpu.get_barrier_semaphore()

    def peer_of(step):
        other = lax.rem(chip + step, chips)
        return other, other * 2 + core

    for peer in [lax.rem(rank + step, ranks) for step in range(1, ranks)]:
        pl.semaphore_signal(
            barrier,
            inc=1,
            device_id={"group": group, "tensor": peer},
            device_id_type=pl.DeviceIdType.MESH,
        )
    key_old = pltpu.make_async_copy(cache_keys, old_keys, old_sems.at[0])
    value_old = pltpu.make_async_copy(cache_values, old_values, old_sems.at[1])
    pl.semaphore_wait(barrier, ranks - 1)

    def pair_copy(block):
        return remote(
            partial_scores.at[1 - core, block],
            paired.at[block],
            send_pair.at[block],
            got_pair.at[block],
            group,
            partner,
        )

    def sum_copy(step, block):
        other, peer = peer_of(step)
        return remote(
            chip_sums.at[other, block],
            incoming.at[chip, block],
            send_sum.at[step, block],
            got_sum.at[chip, block],
            group,
            peer,
        )

    def add_pair(block):
        pair_copy(block).wait_recv()
        for step in range(1, chips):
            other, peer = peer_of(step)
            chip_sums[other, block] = partial_scores[core, block, other] + paired[block, other]
            sum_copy(step, block).start()
        chip_sums[chip, block] = partial_scores[core, block, chip] + paired[block, chip]

    lane = lax.broadcasted_iota(jnp.int32, (1, HEAD_WIDTH), 1)
    sign = jnp.where(lane < HEAD_WIDTH // 2, -1.0, 1.0).astype(jnp.float32)

    def score(block, carry):
        slot = lax.rem(block, 2)

        @pl.when(block + 1 < ranks)
        def _():
            key_copy(block + 1, 1 - slot).start()

        key_copy(block, slot).wait()
        span = pl.ds(pl.multiple_of(block * pages, pages), pages)
        big_cos = base_cos[span, :].reshape(pages, 1, HEAD_WIDTH)
        big_sin = base_sin[span, :].reshape(pages, 1, HEAD_WIDTH)
        small_cos = step_cos[...].reshape(1, PAGE, HEAD_WIDTH)
        small_sin = step_sin[...].reshape(1, PAGE, HEAD_WIDTH)
        cosine = (big_cos * small_cos - big_sin * small_sin).reshape(tile, HEAD_WIDTH)
        sine = (big_sin * small_cos + big_cos * small_sin).reshape(tile, HEAD_WIDTH) * sign
        for h in range(kv_heads):
            columns = slice(h * HEAD_WIDTH, (h + 1) * HEAD_WIDTH)
            head = key_tiles[slot, :, columns].astype(jnp.float32)
            turned[:, columns] = (
                head * cosine + pltpu.roll(head, HEAD_WIDTH // 2, 1) * sine
            ).astype(jnp.bfloat16)
        found = lax.dot_general(
            queries[...], turned[...], (((1,), (1,)), ((), ())), preferred_element_type=jnp.float32
        )
        owner = owner_of[block]
        kept = jnp.zeros((heads, tile), jnp.float32)
        for o in range(owners):
            kept = jnp.where(owner == o, found[o * heads : (o + 1) * heads], kept)
        for j in range(ranks):
            partial_scores[j % 2, block, j // 2] = kept[j * local_heads : (j + 1) * local_heads]
        pair_copy(block).start()

        @pl.when(block > 0)
        def _():
            add_pair(block - 1)

        @pl.when(block == 0)
        def _():
            key_old.start()
            value_old.start()

        return carry

    lax.fori_loop(0, ranks, score, 0)
    add_pair(ranks - 1)

    key_old.wait()
    value_old.wait()
    about = jnp.zeros((heads, HEAD_WIDTH), jnp.float32)
    position = rank * context_dev + lax.broadcasted_iota(jnp.int32, (1, context_dev), 1)
    for b in range(rows):
        old_scores = (
            lax.dot_general(
                own_queries[b], old_keys[b], (((1,), (1,)), ((), ())),
                preferred_element_type=jnp.float32,
            )
            * scale
        )
        old_scores = jnp.where(position < limits[b : b + 1, 0:1], old_scores, masked_score)
        old_peak = jnp.max(old_scores, axis=-1, keepdims=True)
        old_exact = jnp.exp(old_scores - old_peak)
        old_total = jnp.sum(old_exact, axis=-1, keepdims=True)
        old_sum = jnp.dot(
            old_exact.astype(jnp.bfloat16), old_values[b], preferred_element_type=jnp.float32
        )
        about = jnp.where(lane == b, old_peak, jnp.where(lane == rows + b, old_total, about))
        for j in range(ranks):
            h = j * local_heads // per_kv
            old_own[j, b] = old_sum[
                j * local_heads : (j + 1) * local_heads, h * HEAD_WIDTH : (h + 1) * HEAD_WIDTH
            ]
    for j in range(ranks):
        old_own[j, rows] = about[j * local_heads : (j + 1) * local_heads]

    def old_copy(step):
        peer = lax.rem(rank + step, ranks)
        return remote(
            old_own.at[peer], old.at[rank], send_old.at[step], got_old.at[rank], group, peer
        )

    for step in range(1, ranks):
        old_copy(step).start()
    old[rank] = old_own[rank]

    for step in range(1, chips):
        other, peer = peer_of(step)

        def arrive(block, carry):
            remote(
                chip_sums.at[other, block],
                incoming.at[other, block],
                send_sum.at[step, block],
                got_sum.at[other, block],
                group,
                peer,
            ).wait_recv()
            return carry

        lax.fori_loop(0, ranks, arrive, 0)
    total = chip_sums[chip]
    for step in range(1, chips):
        total = total + incoming[peer_of(step)[0]]
    total = total * scale
    owner = owner_of[...]
    peaks = []
    token_peak = jnp.zeros_like(total)
    for o in range(owners):
        kept = jnp.where(owner == o, total, masked_score)
        peak = jnp.max(jnp.max(kept, axis=0), axis=-1, keepdims=True)
        peaks.append(peak)
        token_peak = jnp.where(owner == o, peak[None], token_peak)
    exact = jnp.exp(total - token_peak)
    weights[rank] = exact.astype(jnp.bfloat16)

    def weight_copy(step):
        other, peer = peer_of(step)
        return remote(
            weights.at[rank], weights.at[rank], send_weight.at[step], got_weight.at[rank], group, peer
        )

    def on_copy(step):
        other, peer = peer_of(step)
        return remote(
            weights.at[peer], weights.at[peer], send_on.at[step], got_weight.at[peer], group, partner
        )

    for step in range(1, chips):
        weight_copy(step).start()
    on_copy(0).start()
    for o in range(owners):
        amount = jnp.sum(
            jnp.sum(jnp.where(owner == o, exact, 0.0), axis=0), axis=-1, keepdims=True
        )
        stats[o] = jnp.where(lane == 0, peaks[o], jnp.where(lane == 1, amount, 0.0))
    for step in range(1, chips):
        other, peer = peer_of(step)
        remote(
            weights.at[peer], weights.at[peer], send_weight.at[step], got_weight.at[peer], group, peer
        ).wait_recv()
        on_copy(step).start()
    for step in range(chips):
        other = lax.rem(chip + step, chips) * 2 + 1 - core
        remote(
            weights.at[other], weights.at[other], send_on.at[step], got_weight.at[other], group, partner
        ).wait_recv()

    def sent(block, carry):
        pair_copy(block).wait_send()
        for step in range(1, chips):
            sum_copy(step, block).wait_send()
        return carry

    lax.fori_loop(0, ranks, sent, 0)
    for step in range(1, ranks):
        source = lax.rem(rank + step, ranks)
        remote(
            old_own.at[source], old.at[source], send_old.at[step], got_old.at[source], group, source
        ).wait_recv()
        old_copy(step).wait_send()
    for step in range(chips):
        on_copy(step).wait_send()
        if step:
            weight_copy(step).wait_send()


def fresh_weights(
    ranks, owners, scale, keys, queries, base_cos, base_sin, step_cos, step_sin, owner_of,
    cache_keys, cache_values, own_queries, limits,
):
    tokens, width = keys.shape
    tile = tokens // ranks
    rows, heads = own_queries.shape[:2]
    local_heads = heads // ranks
    chips = ranks // 2
    dma = pltpu.SemaphoreType.DMA
    vmem = pl.BlockSpec(memory_space=pltpu.VMEM)
    hbm = pl.BlockSpec(memory_space=pltpu.HBM)
    held = (chips, local_heads, tile)
    return pl.pallas_call(
        functools.partial(weight_kernel, ranks, owners, scale),
        in_specs=[hbm] + [vmem] * 6 + [hbm] * 2 + [vmem] * 2,
        out_specs=[vmem] * 3,
        out_shape=[
            jax.ShapeDtypeStruct((ranks, ranks, local_heads, tile), jnp.bfloat16),
            jax.ShapeDtypeStruct((owners, local_heads, HEAD_WIDTH), jnp.float32),
            jax.ShapeDtypeStruct((ranks, rows + 1, local_heads, HEAD_WIDTH), jnp.float32),
        ],
        scratch_shapes=[
            pltpu.VMEM((2, ranks) + held, jnp.float32),
            pltpu.VMEM((ranks,) + held, jnp.float32),
            pltpu.VMEM((chips, ranks, local_heads, tile), jnp.float32),
            pltpu.VMEM((chips, ranks, local_heads, tile), jnp.float32),
            pltpu.VMEM((2, tile, width), jnp.bfloat16),
            pltpu.VMEM((tile, width), jnp.bfloat16),
            pltpu.VMEM(cache_keys.shape, jnp.bfloat16),
            pltpu.VMEM(cache_values.shape, jnp.bfloat16),
            pltpu.VMEM((ranks, rows + 1, local_heads, HEAD_WIDTH), jnp.float32),
            dma((ranks,)), dma((chips, ranks)), dma((chips,)), dma((chips,)),
            dma((ranks,)), dma((chips, ranks)), dma((ranks,)), dma((2,)), dma((2,)),
            dma((ranks,)), dma((ranks,)),
        ],
        compiler_params=pltpu.CompilerParams(
            collective_id=1, has_side_effects=True, vmem_limit_bytes=60 * 1024 * 1024
        ),
    )(
        keys, queries, base_cos, base_sin, step_cos, step_sin, owner_of,
        cache_keys, cache_values, own_queries, limits,
    )


def blend_kernel(
    groups, ranks, senders, fresh, stats, old_in, out, fresh_in, stats_in,
    send_fresh, send_stats, got_fresh, got_stats,
):
    group, rank = lax.axis_index("group"), lax.axis_index("tensor")
    rows = out.shape[0]
    count = groups * ranks
    own = group * ranks + rank
    greet_all(groups, ranks, group, rank)

    def peer_of(step):
        peer = lax.rem(own + step, count)
        return peer // ranks, lax.rem(peer, ranks)

    def fresh_copy(step):
        peer_group, peer_rank = peer_of(step)
        return remote(
            fresh.at[peer_group, peer_rank],
            fresh_in.at[group, rank],
            send_fresh.at[step],
            got_fresh.at[group, rank],
            peer_group,
            peer_rank,
        )

    def stats_copy(step):
        peer = lax.rem(group + step, groups)
        return remote(
            stats.at[peer], stats_in.at[group], send_stats.at[step], got_stats.at[group], peer, rank
        )

    for step in range(1, groups):
        stats_copy(step).start()

    def start(step, carry):
        fresh_copy(step).start()
        return carry

    lax.fori_loop(1, count, start, 0)
    stats_in[group] = stats[group]
    fresh_in[group, rank] = fresh[group, rank]
    for step in range(1, groups):
        source = lax.rem(group + step, groups)
        remote(
            stats.at[source], stats_in.at[source], send_stats.at[step], got_stats.at[source], source, rank
        ).wait_recv()

    def finish(step, carry):
        source_group, source_rank = peer_of(step)
        remote(
            fresh.at[source_group, source_rank],
            fresh_in.at[source_group, source_rank],
            send_fresh.at[step],
            got_fresh.at[source_group, source_rank],
            source_group,
            source_rank,
        ).wait_recv()
        fresh_copy(step).wait_send()
        return carry

    lax.fori_loop(1, count, finish, 0)
    for row in range(rows):
        peaks, totals, sums = [], [], []
        for t in range(ranks):
            about = old_in[t, rows]
            peaks.append(about[:, row : row + 1])
            totals.append(about[:, rows + row : rows + row + 1])
            sums.append(old_in[t, row])
        for sender in range(row * senders, (row + 1) * senders):
            about = stats_in[sender]
            peaks.append(about[:, 0:1])
            totals.append(about[:, 1:2])
            sums.append(jnp.sum(fresh_in[sender], axis=0))
        top = functools.reduce(jnp.maximum, peaks)
        factors = [jnp.exp(peak - top) for peak in peaks]
        numerator = sum(a * b for a, b in zip(sums, factors))
        denominator = sum(a * b for a, b in zip(totals, factors))
        out[row] = (numerator / denominator).astype(out.dtype)
    for step in range(1, groups):
        stats_copy(step).wait_send()


def blend(senders, fresh, stats, old):
    groups, ranks, local_heads, width = fresh.shape
    rows = old.shape[1] - 1
    dma = pltpu.SemaphoreType.DMA
    vmem = pl.BlockSpec(memory_space=pltpu.VMEM)
    return pl.pallas_call(
        functools.partial(blend_kernel, groups, ranks, senders),
        in_specs=[vmem] * 3,
        out_specs=vmem,
        out_shape=jax.ShapeDtypeStruct((rows, local_heads, width), jnp.bfloat16),
        scratch_shapes=[
            pltpu.VMEM(fresh.shape, jnp.float32),
            pltpu.VMEM(stats.shape, jnp.float32),
            dma((groups * ranks,)), dma((groups,)), dma((groups, ranks)), dma((groups,)),
        ],
        compiler_params=pltpu.CompilerParams(collective_id=2, has_side_effects=True),
    )(fresh, stats, old)


def per_device(
    prefill_states,
    key_weight,
    value_weight,
    page_slot,
    decode_states,
    query_weight,
    cache_keys,
    cache_values,
    cached_length,
):
    groups = lax.axis_size("group")
    ranks = lax.axis_size("tensor")
    group = lax.axis_index("group")
    rank = lax.axis_index("tensor")
    tokens, features = prefill_states.shape
    fresh_count = tokens // ranks
    pages = fresh_count // PAGE
    kv_heads = key_weight.shape[1] // HEAD_WIDTH
    rows = decode_states.shape[0]
    share = fresh_count // groups
    span = fresh_count // rows
    senders = span // share
    assert senders * share == span
    own_row = group // senders
    offset = (group % senders) * share
    inv_scale = 1.0 / HEAD_WIDTH**0.5

    local_queries = jnp.dot(decode_states, query_weight, preferred_element_type=jnp.float32)
    local_heads = local_queries.shape[1] // HEAD_WIDTH
    heads = local_heads * ranks
    per_kv = heads // kv_heads
    local_queries = apply_rotary(
        local_queries.reshape(rows, local_heads, HEAD_WIDTH),
        (cached_length + ranks * span)[:, None],
    ).astype(jnp.bfloat16)
    pad = jnp.zeros((1, HEAD_WIDTH), jnp.int32)
    meta = jnp.concatenate(
        [
            pad.at[0, :pages].set(page_slot.reshape(pages)),
            pad.at[0, :rows].set(cached_length),
            jnp.zeros((6, HEAD_WIDTH), jnp.int32),
        ],
        axis=0,
    )
    own_query, fresh_query, meta_ranks, meta_groups, keys = gather_queries(
        groups, ranks, senders, local_queries, meta, prefill_states, key_weight
    )
    slots = meta_ranks[:, 0, :pages]
    every_length = meta_groups[:, 1, :rows]

    per_owner = pages // groups
    fresh_length = lax.dynamic_index_in_dim(every_length, own_row, 1, keepdims=False)
    page_owner = slots // per_owner
    length_of_page = jnp.sum(
        jnp.where(
            page_owner[..., None] == jnp.arange(groups, dtype=jnp.int32), fresh_length, 0
        ),
        axis=-1,
    )
    base = (
        length_of_page
        + jnp.arange(ranks, dtype=jnp.int32)[:, None] * span
        + offset
        + (slots % per_owner) * PAGE
    )
    base_cos, base_sin = full_tables(base.reshape(-1))
    step_cos, step_sin = full_tables(jnp.arange(PAGE, dtype=jnp.int32))
    owner_of = jnp.repeat(page_owner, PAGE, axis=1).reshape(ranks, 1, fresh_count)
    own_kv = (jnp.arange(heads) // per_kv)[:, None] == jnp.arange(kv_heads)[None, :]

    def spread(query):
        query = query.reshape(-1, heads, 1, HEAD_WIDTH)
        query = jnp.where(own_kv[None, :, :, None], query, jnp.zeros_like(query))
        return query.reshape(-1, heads, kv_heads * HEAD_WIDTH)

    weights, fresh_stats, old_all = fresh_weights(
        ranks,
        groups,
        inv_scale,
        keys,
        spread(fresh_query).reshape(groups * heads, kv_heads * HEAD_WIDTH),
        base_cos,
        base_sin,
        step_cos,
        step_sin,
        owner_of,
        cache_keys,
        cache_values,
        spread(own_query.transpose(1, 0, 2, 3)),
        jnp.broadcast_to(cached_length[:, None], (rows, HEAD_WIDTH)),
    )

    weights = weights.transpose(0, 2, 1, 3).reshape(heads, tokens)
    owned = owner_of.reshape(1, 1, tokens) == jnp.arange(groups, dtype=jnp.int32)[:, None, None]
    weights = jnp.where(owned, weights[None], jnp.zeros_like(weights)[None])
    mixed = jnp.dot(
        weights.reshape(groups * heads, tokens),
        prefill_states,
        preferred_element_type=jnp.float32,
    )
    fresh_sum = jnp.einsum(
        "oknf,fkd->oknd",
        mixed.astype(jnp.bfloat16).reshape(groups, kv_heads, per_kv, features),
        value_weight.reshape(features, kv_heads, HEAD_WIDTH),
        preferred_element_type=jnp.float32,
    ).reshape(groups, ranks, local_heads, HEAD_WIDTH)

    result = blend(senders, fresh_sum, fresh_stats, old_all)
    return result.reshape(rows, local_heads * HEAD_WIDTH)


def solution(mesh):
    placed = (
        P("group", "tensor"),
        P("tensor", None),
        P("tensor", None),
        P("group", "tensor", None),
        P("group", None),
        P(None, "tensor"),
        P("group", "tensor", None),
        P("group", "tensor", None),
        P("group"),
    )
    return jax.shard_map(
        per_device, mesh=mesh, in_specs=placed, out_specs=P("group", "tensor"), check_vma=False
    )
```
